32 devices in a mesh: rep: 16 (over z, y, x), section: 2 (over core).
Axes of the slice: x: 2, y: 2, z: 4, core: 2. Of those that a mesh axis runs over, the one named last changes fastest.
Arguments:
- ends: bfloat16 [2, 16, 2, 128, 1024], P('section', 'rep'), may hold values from -6 to 6
- w_gate: bfloat16 [2, 16, 1024, 256], P('section', 'rep'), may hold values from -6 to 6
- w_up: bfloat16 [2, 16, 1024, 256], P('section', 'rep'), may hold values from -6 to 6
- slow_down: bfloat16 [2, 16, 256, 1024], P('section', 'rep'), may hold values from -6 to 6
- adam_m: bfloat16 [2, 16, 256, 1024], P('section', 'rep'), may hold values from -2 to 2
- adam_v: bfloat16 [2, 16, 256, 1024], P('section', 'rep'), may hold values from 0.019897461 to 0.19921875
- momentum: bfloat16 [2, 16, 256, 1024], P('section', 'rep'), may hold values from -6 to 6
- routes: int32 [2, 16], replicated, may hold values from 0 to 15, as said below
- partner: int32 [16], replicated, may hold values from 0 to 15, as said below
Outputs:
- new_slow: bfloat16 [2, 16, 256, 1024], P('section', 'rep')
- new_momentum: bfloat16 [2, 16, 256, 1024], P('section', 'rep')
The draws below stay inside these ranges and needn't reach their ends.
Inputs may be any that keep to these rules, and one draw needn't show every extreme that they name: For each micro-batch b there is one number k_b with 1 <= k_b < 16, and routes[b, r] is r with the bits of k_b flipped (bitwise exclusive or). partner[r] is r with the bits of one number of 1 to 3 flipped, the same number for the four replicas of each aligned group of four, so partner[partner[r]] = r.
All inputs are finite; a program needn't handle non-finite values.
Results may differ from the reference program's by a relative error of at most 0.0036.
Values may be sent and summed in bfloat16 or wider, within the bound.
A program may use at most 64 MiB of HBM per device.

```python
import math
import jax
import jax.numpy as jnp
from jax import lax

D = 1024
H = 256
ROWS = 128
MB = 2
REP = 16
SECTIONS = 2


def draw_routes(key, part):
    route_keys = jax.random.randint(jax.random.fold_in(key, 11), (MB,), 1, REP, dtype=jnp.int32)
    replica_ids = jnp.arange(REP, dtype=jnp.int32)
    return jnp.bitwise_xor(replica_ids[None, :], route_keys[:, None]).astype(jnp.int32)


def draw_partner(key, part):
    group_flips = jax.random.randint(jax.random.fold_in(key, 23), (REP // 4,), 1, 4, dtype=jnp.int32)
    replica_ids = jnp.arange(REP, dtype=jnp.int32)
    return jnp.bitwise_xor(replica_ids, group_flips[replica_ids // 4]).astype(jnp.int32)


def steps_of(rng, dims, shards, least, high):
    level, own = 1.0, jax.random.fold_in(rng, 6)
    for dim, parts in shards:
        draws = jnp.exp(jax.random.uniform(jax.random.fold_in(own, dim), (parts,), jnp.float32, least / len(shards), high / len(shards)))
        level = level * jnp.repeat(draws, dims[dim] // parts).reshape([-1 if axis == dim else 1 for axis in range(len(dims))])
    return level


def noise(stream_key, extent, width, bound, shards=(), kind=jnp.bfloat16):
    factor_of = steps_of(stream_key, extent, shards, -0.22, 0.18) if shards else 1.0
    entries = jax.random.normal(stream_key, extent, jnp.float32) * width * factor_of
    return jnp.minimum(jnp.maximum(entries, -bound), bound).astype(kind)


def setup_inputs(seed: int = 0) -> dict:
    streams_of = jax.random.split(jax.random.key(seed), 10)
    return {
        "ends": noise(streams_of[0], (SECTIONS, REP, MB, ROWS, D), 1.0, 6.0, ((0, 2), (1, 16))),
        "w_gate": noise(streams_of[1], (SECTIONS, REP, D, H), 1.0, 6.0, ((0, 2), (1, 16))),
        "w_up": noise(streams_of[2], (SECTIONS, REP, D, H), 1.0, 6.0, ((0, 2), (1, 16))),
        "slow_down": noise(streams_of[3], (SECTIONS, REP, H, D), 1.0, 6.0, ((0, 2), (1, 16))),
        "adam_m": noise(streams_of[4], (SECTIONS, REP, H, D), 0.15, 2.0, ((0, 2), (1, 16))),
        "adam_v": jnp.clip(jnp.exp(math.log(0.19921875) - 2.3038113 * jax.random.uniform(streams_of[5], (SECTIONS, REP, H, D), jnp.float32) ** steps_of(streams_of[5], (SECTIONS, REP, H, D), ((0, 2), (1, 16)), -0.2, 0.2)), 0.019897461, 0.19921875).astype(jnp.bfloat16),
        "momentum": noise(streams_of[6], (SECTIONS, REP, H, D), 1.0, 6.0, ((0, 2), (1, 16))),
        "routes": draw_routes(jax.random.fold_in(streams_of[9], 71), 0),
        "partner": draw_partner(jax.random.fold_in(streams_of[9], 71), 0),
    }


def forward_rows(in_rows, w_gate, w_up, w_down):
    model_width = in_rows.shape[1]
    hidden_units = w_gate.shape[1]
    as_float = in_rows.astype(jnp.float32)
    row_scale = lax.rsqrt(lax.optimization_barrier(jnp.mean(as_float * as_float, axis=1, keepdims=True)) + 1e-06)
    normed = (as_float * row_scale).astype(jnp.bfloat16)
    gate_act = jnp.dot(normed, w_gate, preferred_element_type=jnp.float32) * model_width ** (-0.5)
    up_act = jnp.dot(normed, w_up, preferred_element_type=jnp.float32) * model_width ** (-0.5)
    hidden = (jax.nn.silu(gate_act) * up_act).astype(jnp.bfloat16)
    branch = jnp.dot(hidden, w_down, preferred_element_type=jnp.float32) * hidden_units ** (-0.5)
    result = (as_float + branch).astype(jnp.bfloat16)
    return (result, (row_scale, gate_act, up_act, hidden))

def backward_rows(cotangent, in_rows, saved_state, w_gate, w_up, w_down):
    row_scale, gate_act, up_act, hidden = saved_state
    model_width = in_rows.shape[1]
    hidden_units = w_gate.shape[1]
    d_hidden = jnp.dot(cotangent, w_down.T, preferred_element_type=jnp.float32) * hidden_units ** (-0.5)
    grad_term = jnp.dot(hidden.T, cotangent, preferred_element_type=jnp.float32) * hidden_units ** (-0.5)
    sigmoid_gate = jax.nn.sigmoid(gate_act)
    d_gate = (d_hidden * up_act * sigmoid_gate * (1.0 + gate_act * (1.0 - sigmoid_gate))).astype(jnp.bfloat16)
    d_up = (d_hidden * gate_act * sigmoid_gate).astype(jnp.bfloat16)
    d_normed = (jnp.dot(d_gate, w_gate.T, preferred_element_type=jnp.float32) + jnp.dot(d_up, w_up.T, preferred_element_type=jnp.float32)) * model_width ** (-0.5)
    as_float = in_rows.astype(jnp.float32)
    back_rows = cotangent.astype(jnp.float32) + row_scale * d_normed - as_float * row_scale ** 3 * lax.optimization_barrier(jnp.mean(d_normed * as_float, axis=1, keepdims=True))
    return (grad_term, back_rows.astype(jnp.bfloat16))

def grad_only(cotangent, saved_state, w_down):
    row_scale, gate_act, up_act, hidden = saved_state
    hidden_units = w_down.shape[0]
    return jnp.dot(hidden.T, cotangent, preferred_element_type=jnp.float32) * hidden_units ** (-0.5)

def reference(ends, w_gate, w_up, slow_down, adam_m, adam_v, momentum, routes, partner):
    count_rep = ends.shape[1]
    micro_count = ends.shape[2]
    rows_each = ends.shape[3]
    model_width = ends.shape[4]
    hidden_units = w_gate.shape[3]

    def flatten(stacked):
        return stacked.reshape(count_rep, micro_count * rows_each, model_width)

    def unflatten(stacked):
        return stacked.reshape(count_rep, micro_count, rows_each, model_width)

    def first_forward(operands):
        in_rows, gate_w, up_w, down_w = operands
        return forward_rows(in_rows, gate_w, up_w, down_w)
    sent_rows, first_saved = lax.map(first_forward, (flatten(ends[0]), w_gate[0], w_up[0], slow_down[0]))
    replica_ids = jnp.arange(count_rep, dtype=jnp.int32)
    batch_ids = jnp.arange(micro_count, dtype=jnp.int32)
    inverse = jnp.zeros((micro_count, count_rep), jnp.int32).at[batch_ids[:, None], routes].set(jnp.broadcast_to(replica_ids[None, :], (micro_count, count_rep)))
    arrived = unflatten(sent_rows)[inverse.T, batch_ids[None, :]]

    def last_step(operands):
        in_rows, cotangent, gate_w, up_w, down_w = operands
        result, saved_state = forward_rows(in_rows, gate_w, up_w, down_w)
        return backward_rows(cotangent, in_rows, saved_state, gate_w, up_w, down_w)
    last_grad, back_rows = lax.map(last_step, (flatten(arrived), flatten(ends[1]), w_gate[1], w_up[1], slow_down[1]))
    returned = unflatten(back_rows)[routes.T, batch_ids[None, :]]

    def first_back(operands):
        cotangent, row_scale, gate_act, up_act, hidden, down_w = operands
        return grad_only(cotangent, (row_scale, gate_act, up_act, hidden), down_w)
    first_grad = lax.map(first_back, (flatten(returned),) + tuple(first_saved) + (slow_down[0],))
    grads = jnp.stack([first_grad, last_grad]).reshape(2 * count_rep, hidden_units, model_width)

    def adam_step(operands):
        grad_sum, first_in, second_in, slow_in = operands
        first_moment = 0.9 * first_in.astype(jnp.float32) + 0.1 * grad_sum
        second_moment = 0.999 * second_in.astype(jnp.float32) + 0.001 * grad_sum * grad_sum
        update = first_moment / (jnp.sqrt(second_moment) + 1e-08)
        return (update + 0.1 * slow_in.astype(jnp.float32)).astype(jnp.bfloat16)
    flat_shape = (2 * count_rep, hidden_units, model_width)
    pseudo = lax.map(adam_step, (grads, adam_m.reshape(flat_shape), adam_v.reshape(flat_shape), slow_down.reshape(flat_shape)))
    pseudo = pseudo.reshape(2, count_rep, hidden_units, model_width)

    def outer_step(replica):
        mate = partner[replica]
        mean_pseudo = 0.5 * (pseudo[:, replica].astype(jnp.float32) + pseudo[:, mate].astype(jnp.float32))
        moment = 0.9 * momentum[:, replica].astype(jnp.float32) + mean_pseudo
        averaged = 0.5 * (slow_down[:, replica].astype(jnp.float32) + slow_down[:, mate].astype(jnp.float32))
        updated = averaged - 0.014 * (0.9 * moment + mean_pseudo)
        return (updated.astype(jnp.bfloat16), moment.astype(jnp.bfloat16))
    new_slow, new_momentum = lax.map(outer_step, replica_ids)
    return (jnp.swapaxes(new_slow, 0, 1), jnp.swapaxes(new_momentum, 0, 1))
```

```python
import functools

import jax
import jax.numpy as jnp
from jax import lax
from jax.experimental import pallas as pl
from jax.experimental.pallas import tpu as pltpu
from jax.sharding import PartitionSpec as P


def partner_2(x, axis, bit):
    return lax.ppermute(x, axis, [(i, i ^ 1 << bit) for i in range(lax.axis_size(axis))])


def forward_rows(in_rows, w_gate, w_up, w_down):
    model_width = in_rows.shape[1]
    hidden_units = w_gate.shape[1]
    as_float = in_rows.astype(jnp.float32)
    row_scale = lax.rsqrt(jnp.mean(as_float * as_float, axis=1, keepdims=True) + 1e-06)
    normed = (as_float * row_scale).astype(jnp.bfloat16)
    gate_act = jnp.dot(normed, w_gate, preferred_element_type=jnp.float32) * model_width ** (-0.5)
    up_act = jnp.dot(normed, w_up, preferred_element_type=jnp.float32) * model_width ** (-0.5)
    hidden = (jax.nn.silu(gate_act) * up_act).astype(jnp.bfloat16)
    branch = jnp.dot(hidden, w_down, preferred_element_type=jnp.float32) * hidden_units ** (-0.5)
    result = (as_float + branch).astype(jnp.bfloat16)
    return (result, (row_scale, gate_act, up_act, hidden))


def contract_last(left, right):
    return lax.dot_general(
        left, right, (((1,), (1,)), ((), ())), preferred_element_type=jnp.float32
    )


def grad_rows(cotangent, hidden, hidden_units):
    return lax.dot_general(
        hidden, cotangent, (((0,), (0,)), ((), ())), preferred_element_type=jnp.float32
    ) * hidden_units ** (-0.5)


def backward_rows(cotangent, in_rows, saved_state, w_gate, w_up, w_down):
    row_scale, gate_act, up_act, hidden = saved_state
    model_width = in_rows.shape[1]
    hidden_units = w_gate.shape[1]
    d_hidden = contract_last(cotangent, w_down) * hidden_units ** (-0.5)
    grad_term = grad_rows(cotangent, hidden, hidden_units)
    sigmoid_gate = jax.nn.sigmoid(gate_act)
    d_gate = (d_hidden * up_act * sigmoid_gate * (1.0 + gate_act * (1.0 - sigmoid_gate))).astype(
        jnp.bfloat16
    )
    d_up = (d_hidden * gate_act * sigmoid_gate).astype(jnp.bfloat16)
    d_normed = (contract_last(d_gate, w_gate) + contract_last(d_up, w_up)) * model_width ** (-0.5)
    as_float = in_rows.astype(jnp.float32)
    back_rows = (
        cotangent.astype(jnp.float32)
        + row_scale * d_normed
        - as_float * row_scale**3 * jnp.mean(d_normed * as_float, axis=1, keepdims=True)
    )
    return (grad_term, back_rows.astype(jnp.bfloat16))


def hop_kernel(flip, source, target, rows, out, send_sem, recv_sem):
    me, section = lax.axis_index("rep"), lax.axis_index("section")
    peer = me
    for bit in range(flip.bit_length()):
        if flip >> bit & 1:
            peer = peer + (1 << bit) - (2 << bit) * ((me // (1 << bit)) % 2)
    other = {"rep": peer, "section": section if source == target else 1 - section}
    barrier = pltpu.get_barrier_semaphore()
    pl.semaphore_signal(barrier, inc=1, device_id=other, device_id_type=pl.DeviceIdType.MESH)
    pl.semaphore_wait(barrier, 1)
    copy = pltpu.make_async_remote_copy(
        src_ref=rows, dst_ref=out, send_sem=send_sem, recv_sem=recv_sem,
        device_id=other, device_id_type=pl.DeviceIdType.MESH,
    )

    @pl.when(section == source)
    def _():
        copy.start()
        copy.wait_send()

    @pl.when(section == target)
    def _():
        copy.wait_recv()


def send_rows(payload, flip_key, source):
    bits = lax.axis_size("rep").bit_length() - 1
    starts = list(range(0, bits, 4))
    for index, start in enumerate(starts):
        width = min(4, bits - start)
        target = 1 - source if start == starts[-1] else source

        def branch(flip, index=index, start=start, target=target):
            if target == source and flip == 0:
                return lambda rows: rows
            in_vmem = pl.BlockSpec(memory_space=pltpu.VMEM)
            return pl.pallas_call(
                functools.partial(hop_kernel, flip << start, source, target),
                out_shape=jax.ShapeDtypeStruct(payload.shape, payload.dtype),
                in_specs=[in_vmem],
                out_specs=in_vmem,
                scratch_shapes=[pltpu.SemaphoreType.DMA, pltpu.SemaphoreType.DMA],
                compiler_params=pltpu.CompilerParams(
                    collective_id=1 + (index * 2 + source) * 16 + flip,
                    has_side_effects=True,
                    vmem_limit_bytes=4 * 1024 * 1024,
                ),
                name="hop",
            )

        payload = lax.switch(
            flip_key >> start & (1 << width) - 1, [branch(f) for f in range(1 << width)], payload
        )
    return payload


def outer_kernel(
    chunks, masks, grad, first_in, second_in, slow, mate_slow, momentum,
    new_slow, new_momentum, own, near, chosen, far, send_near, recv_near, send_far, recv_far,
):
    me = lax.axis_index("rep")
    peers = (me + 1 - 2 * (me % 2), me + 2 - 4 * ((me // 2) % 2))
    rows = grad.shape[0] // chunks
    f32, bf16 = jnp.float32, jnp.bfloat16

    barrier = pltpu.get_barrier_semaphore()
    for peer in peers:
        pl.semaphore_signal(
            barrier, inc=1, device_id={"rep": peer}, device_id_type=pl.DeviceIdType.MESH
        )

    def part(c):
        return pl.ds(pl.multiple_of(c * rows, rows), rows)

    def near_copy(c, order):
        return pltpu.make_async_remote_copy(
            src_ref=own.at[part(c)], dst_ref=near.at[part(c)],
            send_sem=send_near.at[c], recv_sem=recv_near.at[c],
            device_id={"rep": peers[order]}, device_id_type=pl.DeviceIdType.MESH,
        )

    def far_copy(c, order):
        return pltpu.make_async_remote_copy(
            src_ref=chosen.at[part(c)], dst_ref=far.at[part(c)],
            send_sem=send_far.at[c], recv_sem=recv_far.at[c],
            device_id={"rep": peers[1 - order]}, device_id_type=pl.DeviceIdType.MESH,
        )

    def adam(c):
        p = part(c)
        g = grad[p, :]
        first = 0.9 * first_in[p, :].astype(f32) + 0.1 * g
        second = 0.999 * second_in[p, :].astype(f32) + 0.001 * g * g
        step = first / (jnp.sqrt(second) + 1e-08)
        own[p, :] = (step + 0.1 * slow[p, :].astype(f32)).astype(bf16)

    def send(c, order):
        near_copy(c, order).start()

    def begin(c, order):
        adam(c)
        send(c, order)

    def pass_on(c, order):
        p = part(c)
        near_copy(c, order).wait_recv()
        chosen[p, :] = jnp.where(
            masks[order : order + 1, :] == 1, near[p, :].astype(f32), own[p, :].astype(f32)
        ).astype(bf16)
        far_copy(c, order).start()

    def finish(c, order):
        p = part(c)
        far_copy(c, order).wait_recv()
        mate = jnp.where(
            masks[1 - order : 2 - order, :] == 1, far[p, :].astype(f32), chosen[p, :].astype(f32)
        )
        mean = 0.5 * (own[p, :].astype(f32) + mate)
        moment = 0.9 * momentum[p, :].astype(f32) + mean
        averaged = 0.5 * (slow[p, :].astype(f32) + mate_slow[p, :].astype(f32))
        new_slow[p, :] = (averaged - 0.014 * (0.9 * moment + mean)).astype(bf16)
        new_momentum[p, :] = moment.astype(bf16)

    def settle(c, order):
        near_copy(c, order).wait_send()
        far_copy(c, order).wait_send()

    def both(start, stop, *stages):
        def run(pair, carry):
            for stage in stages:
                for order in range(2):
                    stage(2 * pair + order, order)
            return carry

        lax.fori_loop(start, stop, run, 0)

    pairs = chunks // 2
    both(0, 1, lambda c, order: adam(c))
    pl.semaphore_wait(barrier, 2)
    both(0, 1, send)
    both(1, pairs, begin)
    both(0, 1, pass_on)
    both(1, pairs, pass_on, lambda c, order: finish(c - 2, order))
    both(pairs - 1, pairs, finish)
    both(0, pairs, settle)


def outer_update(masks, grad, first_in, second_in, slow, mate_slow, momentum):
    hidden_units, model_width = grad.shape
    chunks = hidden_units // 32
    block = pltpu.VMEM((hidden_units, model_width), jnp.bfloat16)
    sems = pltpu.SemaphoreType.DMA((chunks,))
    out = jax.ShapeDtypeStruct((hidden_units, model_width), jnp.bfloat16)
    in_vmem = pl.BlockSpec(memory_space=pltpu.VMEM)
    return pl.pallas_call(
        functools.partial(outer_kernel, chunks),
        out_shape=(out, out),
        in_specs=[in_vmem] * 7,
        out_specs=(in_vmem, in_vmem),
        scratch_shapes=[block] * 4 + [sems] * 4,
        compiler_params=pltpu.CompilerParams(
            collective_id=0, has_side_effects=True, vmem_limit_bytes=16 * 1024 * 1024
        ),
        name="outer",
    )(masks, grad, first_in, second_in, slow, mate_slow, momentum)


def normed_parts(x, gate_w, up_w):
    model_width = x.shape[1]
    row_scale = lax.rsqrt(jnp.mean(x * x, axis=1, keepdims=True) + 1e-06)
    normed = (x * row_scale).astype(jnp.bfloat16)
    scale = model_width ** (-0.5)
    gate_act = jnp.dot(normed, gate_w, preferred_element_type=jnp.float32) * scale
    up_act = jnp.dot(normed, up_w, preferred_element_type=jnp.float32) * scale
    return row_scale, gate_act, up_act


def flipped(me, flip):
    peer = me
    for bit in range(flip.bit_length()):
        if flip >> bit & 1:
            peer = peer + (1 << bit) - (2 << bit) * ((me // (1 << bit)) % 2)
    return peer


def section_one_rows(x, dy, d_hidden, gate_w, up_w):
    bf16 = jnp.bfloat16
    row_scale, gate_act, up_act = normed_parts(x, gate_w, up_w)
    sigmoid_gate = jax.nn.sigmoid(gate_act)
    hidden = (gate_act * sigmoid_gate * up_act).astype(bf16)
    d_gate = d_hidden * up_act * sigmoid_gate * (1.0 + gate_act * (1.0 - sigmoid_gate))
    d_up = d_hidden * gate_act * sigmoid_gate
    d_normed = (
        contract_last(d_gate.astype(bf16), gate_w) + contract_last(d_up.astype(bf16), up_w)
    ) * x.shape[1] ** (-0.5)
    back = (
        dy
        + row_scale * d_normed
        - x * row_scale**3 * jnp.mean(d_normed * x, axis=1, keepdims=True)
    )
    return hidden, back.astype(bf16)


def keys_kernel(micro_count, routes, partner, *outs):
    me = lax.axis_index("rep")
    for b in range(micro_count):
        outs[b][0] = routes[b, 0] - 1
    outs[micro_count][0] = jnp.bitwise_xor(partner[me], me)


def read_keys(routes, partner):
    in_smem = pl.BlockSpec(memory_space=pltpu.SMEM)
    count = routes.shape[0] + 1
    return pl.pallas_call(
        functools.partial(keys_kernel, routes.shape[0]),
        out_shape=[jax.ShapeDtypeStruct((1,), jnp.int32)] * count,
        in_specs=[in_smem] * 2,
        out_specs=[in_smem] * count,
        name="keys",
    )(routes, partner)


def first_kernel(
    flip, chunk, bits, ends, gate_h, up_h, slow_h,
    gate, up, slow, mate, hidden, dy, sent,
    x, dh, near, chosen, far,
    load_sem, row_sem, go_send, go_recv, come_send, come_recv,
    near_send, near_recv, far_send, far_recv,
):
    me, section = lax.axis_index("rep"), lax.axis_index("section")
    f32, bf16 = jnp.float32, jnp.bfloat16
    mesh_ids = pl.DeviceIdType.MESH
    rows, _ = dy.shape
    units = slow.shape[0]
    per_batch = rows // chunk
    other = {"rep": flipped(me, flip), "section": 1 - section}
    peers = (flipped(me, 1), flipped(me, 2))
    half = units // 2

    barrier = pltpu.get_barrier_semaphore()
    pl.semaphore_signal(barrier, inc=1, device_id=other, device_id_type=mesh_ids)
    for peer in peers:
        pl.semaphore_signal(barrier, inc=1, device_id={"rep": peer}, device_id_type=mesh_ids)

    loads = [
        pltpu.make_async_copy(source, target, load_sem.at[i])
        for i, (source, target) in enumerate(((gate_h, gate), (up_h, up), (slow_h, slow)))
    ]
    load_x = pltpu.make_async_copy(ends, x, row_sem.at[0])
    load_dy = pltpu.make_async_copy(ends.at[pl.ds(0, rows)], dy, row_sem.at[1])

    @pl.when(section == 0)
    def _():
        load_x.start()

    @pl.when(section == 1)
    def _():
        load_dy.start()

    for load in loads:
        load.start()

    def span(c):
        return pl.ds(pl.multiple_of(c * chunk, chunk), chunk)

    def going(c):
        return pltpu.make_async_remote_copy(
            src_ref=sent.at[span(c)], dst_ref=x.at[span(c)],
            send_sem=go_send.at[c], recv_sem=go_recv.at[c],
            device_id=other, device_id_type=mesh_ids,
        )

    def coming(c):
        return pltpu.make_async_remote_copy(
            src_ref=sent.at[span(c)], dst_ref=dy.at[span(c)],
            send_sem=come_send.at[c], recv_sem=come_recv.at[c],
            device_id=other, device_id_type=mesh_ids,
        )

    def near_copy(order):
        return pltpu.make_async_remote_copy(
            src_ref=slow.at[pl.ds(order * half, half)], dst_ref=near.at[order],
            send_sem=near_send.at[order], recv_sem=near_recv.at[order],
            device_id={"rep": peers[order]}, device_id_type=mesh_ids,
        )

    def far_copy(order):
        return pltpu.make_async_remote_copy(
            src_ref=chosen.at[order], dst_ref=far.at[order],
            send_sem=far_send.at[order], recv_sem=far_recv.at[order],
            device_id={"rep": peers[1 - order]}, device_id_type=mesh_ids,
        )

    flags = [(bits[0] // (1 << order)) % 2 == 1 for order in range(2)]

    @pl.when(section == 1)
    def _():
        load_dy.wait()

    @pl.when(section == 0)
    def _():
        load_x.wait()

    for load in loads:
        load.wait()

    @pl.when(section == 1)
    def _():
        dh[...] = contract_last(dy[...], slow[...]) * units ** (-0.5)

    last = jnp.where(section == 0, 2 * per_batch, per_batch)

    def body(c, carry):
        @pl.when(jnp.logical_and(section == 1, c == 0))
        def _():
            pl.semaphore_wait(barrier, 3)
            near_copy(0).start()
            near_copy(1).start()

        @pl.when(c == last - 1)
        def _():
            for order in range(2):
                near_copy(order).wait_recv()
                chosen[order] = jnp.where(
                    flags[order],
                    near[order].astype(f32),
                    slow[pl.ds(order * half, half), :].astype(f32),
                ).astype(bf16)
                far_copy(order).start()

        @pl.when(section == 1)
        def _():
            going(c).wait_recv()
            hid, back = section_one_rows(
                x[span(c), :].astype(f32), dy[span(c), :].astype(f32), dh[span(c), :],
                gate[...], up[...],
            )
            hidden[span(c), :] = hid
            sent[span(c), :] = back
            coming(c).start()

        @pl.when(section == 0)
        def _():
            as_float = x[span(c), :].astype(f32)
            _, gate_act, up_act = normed_parts(as_float, gate[...], up[...])
            hid = (jax.nn.silu(gate_act) * up_act).astype(bf16)
            hidden[span(c), :] = hid
            branch = jnp.dot(hid, slow[...], preferred_element_type=f32) * units ** (-0.5)
            sent[span(c), :] = (as_float + branch).astype(bf16)

        @pl.when(jnp.logical_and(section == 0, c == 0))
        def _():
            pl.semaphore_wait(barrier, 3)

        @pl.when(jnp.logical_and(section == 0, c < per_batch))
        def _():
            going(c).start()

        @pl.when(jnp.logical_and(section == 0, c == per_batch - 1))
        def _():
            near_copy(0).start()
            near_copy(1).start()

        return carry

    lax.fori_loop(0, last, body, 0)

    for order in range(2):
        far_copy(order).wait_recv()
        mate[pl.ds(order * half, half), :] = jnp.where(
            flags[1 - order], far[order].astype(f32), chosen[order].astype(f32)
        ).astype(bf16)
        near_copy(order).wait_send()
        far_copy(order).wait_send()

    @pl.when(section == 1)
    def _():
        for c in range(per_batch):
            coming(c).wait_send()

    @pl.when(section == 0)
    def _():
        for c in range(per_batch):
            going(c).wait_send()
        for c in range(per_batch):
            coming(c).wait_recv()


def first_trip(flip, chunk, bits, ends, gate_w, up_w, slow):
    model_width, units = gate_w.shape
    rows = ends.shape[0] // 2
    count = rows // chunk
    bf16, f32 = jnp.bfloat16, jnp.float32
    shapes = [
        gate_w.shape, up_w.shape, slow.shape, slow.shape,
        (2 * rows, units), (rows, model_width), (2 * rows, model_width),
    ]
    in_vmem = pl.BlockSpec(memory_space=pltpu.VMEM)
    half = pltpu.VMEM((2, units // 2, model_width), bf16)
    dma = pltpu.SemaphoreType.DMA
    return pl.pallas_call(
        functools.partial(first_kernel, flip, chunk),
        out_shape=[jax.ShapeDtypeStruct(shape, bf16) for shape in shapes],
        in_specs=[pl.BlockSpec(memory_space=pltpu.SMEM)]
        + [pl.BlockSpec(memory_space=pl.ANY)] * 4,
        out_specs=[in_vmem] * len(shapes),
        scratch_shapes=[
            pltpu.VMEM((2 * rows, model_width), bf16), pltpu.VMEM((rows, units), f32),
            half, half, half,
            dma((3,)), dma((2,)), dma((count,)), dma((count,)), dma((count,)), dma((count,)),
            dma((2,)), dma((2,)), dma((2,)), dma((2,)),
        ],
        compiler_params=pltpu.CompilerParams(
            collective_id=flip, has_side_effects=True, vmem_limit_bytes=24 * 1024 * 1024
        ),
        name="first",
    )(bits, ends, gate_w, up_w, slow)


def second_kernel(
    flip, chunk, ends, first_h, second_h, momentum_h, gate, up, slow, hidden_in, dy_in, sent,
    hidden_t, dy, first_in, second_in, momentum,
    x, back_rows, hidden, dh,
    load_sem, row_sem, go_send, go_recv, come_send, come_recv,
):
    me, section = lax.axis_index("rep"), lax.axis_index("section")
    f32 = jnp.float32
    mesh_ids = pl.DeviceIdType.MESH
    rows, _ = x.shape
    units = slow.shape[0]
    count = rows // chunk
    other = {"rep": flipped(me, flip), "section": 1 - section}

    barrier = pltpu.get_barrier_semaphore()
    pl.semaphore_signal(barrier, inc=1, device_id=other, device_id_type=mesh_ids)

    loads = [
        pltpu.make_async_copy(source, target, load_sem.at[i])
        for i, (source, target) in enumerate(
            (
                (first_h, first_in), (second_h, second_in), (momentum_h, momentum),
                (dy_in, dy.at[pl.ds(0, rows)]),
            )
        )
    ]
    load_dy = pltpu.make_async_copy(ends.at[pl.ds(rows, rows)], dy.at[pl.ds(rows, rows)], row_sem)

    def span(c, base=0):
        return pl.ds(pl.multiple_of(base + c * chunk, chunk), chunk)

    def going(c):
        return pltpu.make_async_remote_copy(
            src_ref=sent.at[span(c, rows)], dst_ref=x.at[span(c)],
            send_sem=go_send.at[c], recv_sem=go_recv.at[c],
            device_id=other, device_id_type=mesh_ids,
        )

    def coming(c):
        return pltpu.make_async_remote_copy(
            src_ref=back_rows.at[span(c)], dst_ref=dy.at[span(c, rows)],
            send_sem=come_send.at[c], recv_sem=come_recv.at[c],
            device_id=other, device_id_type=mesh_ids,
        )

    @pl.when(section == 1)
    def _():
        load_dy.start()

    pl.semaphore_wait(barrier, 1)

    @pl.when(section == 0)
    def _():
        for c in range(count):
            going(c).start()

    for load in loads:
        load.start()

    @pl.when(section == 0)
    def _():
        hidden[...] = hidden_in[...]

    @pl.when(section == 1)
    def _():
        hidden[pl.ds(0, rows), :] = hidden_in[pl.ds(0, rows), :]
        load_dy.wait()
        dh[...] = contract_last(dy[pl.ds(rows, rows), :], slow[...]) * units ** (-0.5)

        def body(c, carry):
            going(c).wait_recv()
            hid, back = section_one_rows(
                x[span(c), :].astype(f32), dy[span(c, rows), :].astype(f32), dh[span(c), :],
                gate[...], up[...],
            )
            hidden[span(c, rows), :] = hid
            back_rows[span(c), :] = back
            coming(c).start()
            return carry

        lax.fori_loop(0, count, body, 0)

    hidden_t[...] = hidden[...].T
    for load in loads:
        load.wait()

    @pl.when(section == 1)
    def _():
        for c in range(count):
            coming(c).wait_send()

    @pl.when(section == 0)
    def _():
        for c in range(count):
            going(c).wait_send()
        for c in range(count):
            coming(c).wait_recv()


def second_trip(
    flip, chunk, ends, adam_m, adam_v, momentum, gate_w, up_w, slow, hidden, dy, sent
):
    model_width, units = gate_w.shape
    rows = ends.shape[0] // 2
    count = rows // chunk
    bf16, f32 = jnp.bfloat16, jnp.float32
    shapes = [(units, 2 * rows), (2 * rows, model_width)] + [slow.shape] * 3
    in_vmem = pl.BlockSpec(memory_space=pltpu.VMEM)
    dma = pltpu.SemaphoreType.DMA
    return pl.pallas_call(
        functools.partial(second_kernel, flip, chunk),
        out_shape=[jax.ShapeDtypeStruct(shape, bf16) for shape in shapes],
        in_specs=[pl.BlockSpec(memory_space=pl.ANY)] * 4 + [in_vmem] * 6,
        out_specs=[in_vmem] * len(shapes),
        scratch_shapes=[
            pltpu.VMEM((rows, model_width), bf16), pltpu.VMEM((rows, model_width), bf16),
            pltpu.VMEM((2 * rows, units), bf16), pltpu.VMEM((rows, units), f32),
            dma((4,)), dma, dma((count,)), dma((count,)), dma((count,)), dma((count,)),
        ],
        compiler_params=pltpu.CompilerParams(
            collective_id=16 + flip, has_side_effects=True, vmem_limit_bytes=24 * 1024 * 1024
        ),
        name="second",
    )(ends, adam_m, adam_v, momentum, gate_w, up_w, slow, hidden, dy, sent)


def pseudo_kernel(
    bits, hidden_t, dy, first_in, second_in, slow,
    own, mate, near, chosen, far, send_near, recv_near, send_far, recv_far,
):
    me = lax.axis_index("rep")
    peers = (flipped(me, 1), flipped(me, 2))
    chunks, units, width = own.shape
    f32, bf16 = jnp.float32, jnp.bfloat16

    barrier = pltpu.get_barrier_semaphore()
    for peer in peers:
        pl.semaphore_signal(
            barrier, inc=1, device_id={"rep": peer}, device_id_type=pl.DeviceIdType.MESH
        )
    flags = [(bits[0] // (1 << order)) % 2 == 1 for order in range(2)]

    def near_copy(c, order):
        return pltpu.make_async_remote_copy(
            src_ref=own.at[c], dst_ref=near.at[c],
            send_sem=send_near.at[c], recv_sem=recv_near.at[c],
            device_id={"rep": peers[order]}, device_id_type=pl.DeviceIdType.MESH,
        )

    def far_copy(c, order):
        return pltpu.make_async_remote_copy(
            src_ref=chosen.at[c], dst_ref=far.at[c],
            send_sem=send_far.at[c], recv_sem=recv_far.at[c],
            device_id={"rep": peers[1 - order]}, device_id_type=pl.DeviceIdType.MESH,
        )

    def adam(c):
        p = pl.ds(pl.multiple_of(c * width, width), width)
        g = jnp.dot(hidden_t[...], dy[:, p], preferred_element_type=f32) * units ** (-0.5)
        first = 0.9 * first_in[:, p].astype(f32) + 0.1 * g
        second = 0.999 * second_in[:, p].astype(f32) + 0.001 * g * g
        step = first / (jnp.sqrt(second) + 1e-08)
        own[c] = (step + 0.1 * slow[:, p].astype(f32)).astype(bf16)

    def send(c, order):
        near_copy(c, order).start()

    def begin(c, order):
        adam(c)
        send(c, order)

    def pass_on(c, order):
        near_copy(c, order).wait_recv()
        chosen[c] = jnp.where(
            flags[order], near[c].astype(f32), own[c].astype(f32)
        ).astype(bf16)
        far_copy(c, order).start()

    def finish(c, order):
        far_copy(c, order).wait_recv()
        mate[c] = jnp.where(
            flags[1 - order], far[c].astype(f32), chosen[c].astype(f32)
        ).astype(bf16)

    def settle(c, order):
        near_copy(c, order).wait_send()
        far_copy(c, order).wait_send()

    def both(start, stop, *stages):
        def run(pair, carry):
            for stage in stages:
                for order in range(2):
                    stage(2 * pair + order, order)
            return carry

        lax.fori_loop(start, stop, run, 0)

    pairs = chunks // 2
    both(0, 1, lambda c, order: adam(c))
    pl.semaphore_wait(barrier, 2)
    both(0, 1, send)
    both(1, pairs, begin)
    both(0, 1, pass_on)
    both(1, pairs, pass_on, lambda c, order: finish(c - 2, order))
    both(pairs - 1, pairs, finish)
    both(0, pairs, settle)


def pseudo_update(bits, hidden_t, dy, first_in, second_in, slow):
    units, model_width = slow.shape
    width = 128
    chunks = model_width // width
    block = (chunks, units, width)
    sems = pltpu.SemaphoreType.DMA((chunks,))
    out = jax.ShapeDtypeStruct(block, jnp.bfloat16)
    in_vmem = pl.BlockSpec(memory_space=pltpu.VMEM)
    return pl.pallas_call(
        pseudo_kernel,
        out_shape=(out, out),
        in_specs=[pl.BlockSpec(memory_space=pltpu.SMEM)] + [in_vmem] * 5,
        out_specs=(in_vmem, in_vmem),
        scratch_shapes=[pltpu.VMEM(block, jnp.bfloat16)] * 3 + [sems] * 4,
        compiler_params=pltpu.CompilerParams(
            collective_id=0, has_side_effects=True, vmem_limit_bytes=24 * 1024 * 1024
        ),
        name="pseudo",
    )(bits, hidden_t, dy, first_in, second_in, slow)


def last_kernel(own, mate, slow, mate_slow, momentum, new_slow_h, new_momentum_h,
                new_slow, new_momentum, sems):
    chunks, _, width = own.shape
    f32, bf16 = jnp.float32, jnp.bfloat16

    def puts(c):
        p = pl.ds(pl.multiple_of(c * width, width), width)
        return (
            pltpu.make_async_copy(new_slow.at[:, p], new_slow_h.at[:, p], sems.at[0, c]),
            pltpu.make_async_copy(new_momentum.at[:, p], new_momentum_h.at[:, p], sems.at[1, c]),
        )

    def run(c, carry):
        p = pl.ds(pl.multiple_of(c * width, width), width)
        mean = 0.5 * (own[c].astype(f32) + mate[c].astype(f32))
        moment = 0.9 * momentum[:, p].astype(f32) + mean
        averaged = 0.5 * (slow[:, p].astype(f32) + mate_slow[:, p].astype(f32))
        new_slow[:, p] = (averaged - 0.014 * (0.9 * moment + mean)).astype(bf16)
        new_momentum[:, p] = moment.astype(bf16)
        for put in puts(c):
            put.start()
        return carry

    lax.fori_loop(0, chunks, run, 0)

    def settle(c, carry):
        for put in puts(c):
            put.wait()
        return carry

    lax.fori_loop(0, chunks, settle, 0)


def last_step(own, mate, slow, mate_slow, momentum):
    block = pltpu.VMEM(slow.shape, jnp.bfloat16)
    out = jax.ShapeDtypeStruct(slow.shape, jnp.bfloat16)
    in_vmem = pl.BlockSpec(memory_space=pltpu.VMEM)
    anywhere = pl.BlockSpec(memory_space=pl.ANY)
    return pl.pallas_call(
        last_kernel,
        out_shape=(out, out),
        in_specs=[in_vmem] * 5,
        out_specs=(anywhere, anywhere),
        scratch_shapes=[block, block, pltpu.SemaphoreType.DMA((2, own.shape[0]))],
        compiler_params=pltpu.CompilerParams(vmem_limit_bytes=24 * 1024 * 1024),
        name="last",
    )(own, mate, slow, mate_slow, momentum)


def trip_on_device(ends, w_gate, w_up, slow_down, adam_m, adam_v, momentum, routes, partner):
    micro_count, row_count, model_width = ends.shape[2:]
    flat_ends = ends.reshape(micro_count * row_count, model_width)
    gate_w, up_w, down_w = w_gate[0, 0], w_up[0, 0], slow_down[0, 0]
    chunk = row_count // 2
    flips = range(1, lax.axis_size("rep"))
    *keys, bits = read_keys(routes, partner)
    gate_v, up_v, slow_v, mate_slow, hidden, dy, sent = lax.switch(
        keys[0][0],
        [functools.partial(first_trip, flip, chunk) for flip in flips],
        bits, flat_ends, gate_w, up_w, down_w,
    )
    hidden_t, dy, first_in, second_in, momentum_v = lax.switch(
        keys[1][0],
        [functools.partial(second_trip, flip, chunk) for flip in flips],
        flat_ends, adam_m[0, 0], adam_v[0, 0], momentum[0, 0],
        gate_v, up_v, slow_v, hidden, dy, sent,
    )
    own, mate = pseudo_update(bits, hidden_t, dy, first_in, second_in, slow_v)
    new_slow, new_momentum = last_step(own, mate, slow_v, mate_slow, momentum_v)
    return new_slow[None, None], new_momentum[None, None]


def wide_on_device(ends, w_gate, w_up, slow_down, adam_m, adam_v, momentum, routes, partner):
    micro_count, row_count, model_width = ends.shape[2:]
    own_data = ends.reshape(micro_count * row_count, model_width)
    gate_w = w_gate[0, 0]
    up_w = w_up[0, 0]
    down_w = slow_down[0, 0]
    hidden_units = gate_w.shape[1]
    replica = lax.axis_index("rep")
    on_first = lax.axis_index("section") == 0
    flip_keys = routes[:, 0]
    flip_bits = jnp.bitwise_xor(partner[replica], replica)
    near_slow = partner_2(down_w, "rep", 0)

    def cut(rows):
        return rows.reshape(micro_count, row_count, model_width)

    def first_forward():
        result, saved = forward_rows(own_data, gate_w, up_w, down_w)
        return result, saved[3]

    def first_idle():
        return own_data, jnp.zeros((own_data.shape[0], hidden_units), jnp.bfloat16)

    sent, hidden = lax.cond(on_first, first_forward, first_idle)
    sent = cut(sent)
    arrived = [send_rows(sent[b], flip_keys[b], 0) for b in range(micro_count)]
    near_slow, *arrived = lax.optimization_barrier((near_slow, *arrived))
    arrived = jnp.concatenate(arrived)
    chosen_slow = jnp.where(flip_bits & 1 == 1, near_slow, down_w)
    far_slow = partner_2(chosen_slow, "rep", 1)

    def last_work():
        _, saved = forward_rows(arrived, gate_w, up_w, down_w)
        term, back = backward_rows(own_data, arrived, saved, gate_w, up_w, down_w)
        return term, back

    def last_idle():
        return jnp.zeros((hidden_units, model_width), jnp.float32), own_data

    last_term, back = lax.cond(on_first, last_idle, last_work)
    back = cut(back)
    returned = [send_rows(back[b], flip_keys[b], 1) for b in range(micro_count)]
    far_slow, *returned = lax.optimization_barrier((far_slow, *returned))
    returned = jnp.concatenate(returned)
    partner_slow = jnp.where(flip_bits >> 1 & 1 == 1, far_slow, chosen_slow)
    grad_sum = lax.cond(
        on_first, lambda: grad_rows(returned, hidden, hidden_units), lambda: last_term
    )
    masks = jnp.zeros((8, model_width), jnp.int32)
    masks = masks.at[0].set(flip_bits & 1).at[1].set(flip_bits >> 1 & 1)
    new_slow, new_momentum = outer_update(
        masks, grad_sum, adam_m[0, 0], adam_v[0, 0], down_w, partner_slow, momentum[0, 0]
    )
    return new_slow[None, None], new_momentum[None, None]


def solution(mesh):
    weights = P("section", "rep", None, None)
    placed = (P("section", "rep", None, None, None),) + (weights,) * 6 + (P(), P())
    narrow = mesh.shape["rep"] <= 16
    on_device = trip_on_device if narrow else wide_on_device

    return jax.shard_map(
        on_device, mesh=mesh, in_specs=placed, out_specs=(weights, weights), check_vma=False
    )
```

```python
import functools

import jax
import jax.numpy as jnp
from jax import lax
from jax.experimental import pallas as pl
from jax.experimental.pallas import tpu as pltpu
from jax.sharding import PartitionSpec as P


def partner_2(x, axis, bit):
    return lax.ppermute(x, axis, [(i, i ^ 1 << bit) for i in range(lax.axis_size(axis))])


def forward_rows(in_rows, w_gate, w_up, w_down):
    model_width = in_rows.shape[1]
    hidden_units = w_gate.shape[1]
    as_float = in_rows.astype(jnp.float32)
    row_scale = lax.rsqrt(jnp.mean(as_float * as_float, axis=1, keepdims=True) + 1e-06)
    normed = (as_float * row_scale).astype(jnp.bfloat16)
    gate_act = jnp.dot(normed, w_gate, preferred_element_type=jnp.float32) * model_width ** (-0.5)
    up_act = jnp.dot(normed, w_up, preferred_element_type=jnp.float32) * model_width ** (-0.5)
    hidden = (jax.nn.silu(gate_act) * up_act).astype(jnp.bfloat16)
    branch = jnp.dot(hidden, w_down, preferred_element_type=jnp.float32) * hidden_units ** (-0.5)
    result = (as_float + branch).astype(jnp.bfloat16)
    return (result, (row_scale, gate_act, up_act, hidden))


def contract_last(left, right):
    return lax.dot_general(
        left, right, (((1,), (1,)), ((), ())), preferred_element_type=jnp.float32
    )


def grad_rows(cotangent, hidden, hidden_units):
    return lax.dot_general(
        hidden, cotangent, (((0,), (0,)), ((), ())), preferred_element_type=jnp.float32
    ) * hidden_units ** (-0.5)


def backward_rows(cotangent, in_rows, saved_state, w_gate, w_up, w_down):
    row_scale, gate_act, up_act, hidden = saved_state
    model_width = in_rows.shape[1]
    hidden_units = w_gate.shape[1]
    d_hidden = contract_last(cotangent, w_down) * hidden_units ** (-0.5)
    grad_term = grad_rows(cotangent, hidden, hidden_units)
    sigmoid_gate = jax.nn.sigmoid(gate_act)
    d_gate = (d_hidden * up_act * sigmoid_gate * (1.0 + gate_act * (1.0 - sigmoid_gate))).astype(
        jnp.bfloat16
    )
    d_up = (d_hidden * gate_act * sigmoid_gate).astype(jnp.bfloat16)
    d_normed = (contract_last(d_gate, w_gate) + contract_last(d_up, w_up)) * model_width ** (-0.5)
    as_float = in_rows.astype(jnp.float32)
    back_rows = (
        cotangent.astype(jnp.float32)
        + row_scale * d_normed
        - as_float * row_scale**3 * jnp.mean(d_normed * as_float, axis=1, keepdims=True)
    )
    return (grad_term, back_rows.astype(jnp.bfloat16))


def hop_kernel(flip, source, target, rows, out, send_sem, recv_sem):
    me, section = lax.axis_index("rep"), lax.axis_index("section")
    peer = me
    for bit in range(flip.bit_length()):
        if flip >> bit & 1:
            peer = peer + (1 << bit) - (2 << bit) * ((me // (1 << bit)) % 2)
    other = {"rep": peer, "section": section if source == target else 1 - section}
    barrier = pltpu.get_barrier_semaphore()
    pl.semaphore_signal(barrier, inc=1, device_id=other, device_id_type=pl.DeviceIdType.MESH)
    pl.semaphore_wait(barrier, 1)
    copy = pltpu.make_async_remote_copy(
        src_ref=rows, dst_ref=out, send_sem=send_sem, recv_sem=recv_sem,
        device_id=other, device_id_type=pl.DeviceIdType.MESH,
    )

    @pl.when(section == source)
    def _():
        copy.start()
        copy.wait_send()

    @pl.when(section == target)
    def _():
        copy.wait_recv()


def send_rows(payload, flip_key, source):
    bits = lax.axis_size("rep").bit_length() - 1
    starts = list(range(0, bits, 4))
    for index, start in enumerate(starts):
        width = min(4, bits - start)
        target = 1 - source if start == starts[-1] else source

        def branch(flip, index=index, start=start, target=target):
            if target == source and flip == 0:
                return lambda rows: rows
            in_vmem = pl.BlockSpec(memory_space=pltpu.VMEM)
            return pl.pallas_call(
                functools.partial(hop_kernel, flip << start, source, target),
                out_shape=jax.ShapeDtypeStruct(payload.shape, payload.dtype),
                in_specs=[in_vmem],
                out_specs=in_vmem,
                scratch_shapes=[pltpu.SemaphoreType.DMA, pltpu.SemaphoreType.DMA],
                compiler_params=pltpu.CompilerParams(
                    collective_id=1 + (index * 2 + source) * 16 + flip,
                    has_side_effects=True,
                    vmem_limit_bytes=4 * 1024 * 1024,
                ),
                name="hop",
            )

        payload = lax.switch(
            flip_key >> start & (1 << width) - 1, [branch(f) for f in range(1 << width)], payload
        )
    return payload


def outer_kernel(
    chunks, masks, grad, first_in, second_in, slow, mate_slow, momentum,
    new_slow, new_momentum, own, near, chosen, far, send_near, recv_near, send_far, recv_far,
):
    me = lax.axis_index("rep")
    peers = (me + 1 - 2 * (me % 2), me + 2 - 4 * ((me // 2) % 2))
    rows = grad.shape[0] // chunks
    f32, bf16 = jnp.float32, jnp.bfloat16

    barrier = pltpu.get_barrier_semaphore()
    for peer in peers:
        pl.semaphore_signal(
            barrier, inc=1, device_id={"rep": peer}, device_id_type=pl.DeviceIdType.MESH
        )

    def part(c):
        return pl.ds(pl.multiple_of(c * rows, rows), rows)

    def near_copy(c, order):
        return pltpu.make_async_remote_copy(
            src_ref=own.at[part(c)], dst_ref=near.at[part(c)],
            send_sem=send_near.at[c], recv_sem=recv_near.at[c],
            device_id={"rep": peers[order]}, device_id_type=pl.DeviceIdType.MESH,
        )

    def far_copy(c, order):
        return pltpu.make_async_remote_copy(
            src_ref=chosen.at[part(c)], dst_ref=far.at[part(c)],
            send_sem=send_far.at[c], recv_sem=recv_far.at[c],
            device_id={"rep": peers[1 - order]}, device_id_type=pl.DeviceIdType.MESH,
        )

    def adam(c):
        p = part(c)
        g = grad[p, :]
        first = 0.9 * first_in[p, :].astype(f32) + 0.1 * g
        second = 0.999 * second_in[p, :].astype(f32) + 0.001 * g * g
        step = first / (jnp.sqrt(second) + 1e-08)
        own[p, :] = (step + 0.1 * slow[p, :].astype(f32)).astype(bf16)

    def send(c, order):
        near_copy(c, order).start()

    def begin(c, order):
        adam(c)
        send(c, order)

    def pass_on(c, order):
        p = part(c)
        near_copy(c, order).wait_recv()
        chosen[p, :] = jnp.where(
            masks[order : order + 1, :] == 1, near[p, :].astype(f32), own[p, :].astype(f32)
        ).astype(bf16)
        far_copy(c, order).start()

    def finish(c, order):
        p = part(c)
        far_copy(c, order).wait_recv()
        mate = jnp.where(
            masks[1 - order : 2 - order, :] == 1, far[p, :].astype(f32), chosen[p, :].astype(f32)
        )
        mean = 0.5 * (own[p, :].astype(f32) + mate)
        moment = 0.9 * momentum[p, :].astype(f32) + mean
        averaged = 0.5 * (slow[p, :].astype(f32) + mate_slow[p, :].astype(f32))
        new_slow[p, :] = (averaged - 0.014 * (0.9 * moment + mean)).astype(bf16)
        new_momentum[p, :] = moment.astype(bf16)

    def settle(c, order):
        near_copy(c, order).wait_send()
        far_copy(c, order).wait_send()

    def both(start, stop, *stages):
        def run(pair, carry):
            for stage in stages:
                for order in range(2):
                    stage(2 * pair + order, order)
            return carry

        lax.fori_loop(start, stop, run, 0)

    pairs = chunks // 2
    both(0, 1, lambda c, order: adam(c))
    pl.semaphore_wait(barrier, 2)
    both(0, 1, send)
    both(1, pairs, begin)
    both(0, 1, pass_on)
    both(1, pairs, pass_on, lambda c, order: finish(c - 2, order))
    both(pairs - 1, pairs, finish)
    both(0, pairs, settle)


def outer_update(masks, grad, first_in, second_in, slow, mate_slow, momentum):
    hidden_units, model_width = grad.shape
    chunks = hidden_units // 32
    block = pltpu.VMEM((hidden_units, model_width), jnp.bfloat16)
    sems = pltpu.SemaphoreType.DMA((chunks,))
    out = jax.ShapeDtypeStruct((hidden_units, model_width), jnp.bfloat16)
    in_vmem = pl.BlockSpec(memory_space=pltpu.VMEM)
    return pl.pallas_call(
        functools.partial(outer_kernel, chunks),
        out_shape=(out, out),
        in_specs=[in_vmem] * 7,
        out_specs=(in_vmem, in_vmem),
        scratch_shapes=[block] * 4 + [sems] * 4,
        compiler_params=pltpu.CompilerParams(
            collective_id=0, has_side_effects=True, vmem_limit_bytes=16 * 1024 * 1024
        ),
        name="outer",
    )(masks, grad, first_in, second_in, slow, mate_slow, momentum)


def normed_parts(x, gate_w, up_w):
    model_width = x.shape[1]
    row_scale = lax.rsqrt(jnp.mean(x * x, axis=1, keepdims=True) + 1e-06)
    normed = (x * row_scale).astype(jnp.bfloat16)
    scale = model_width ** (-0.5)
    gate_act = jnp.dot(normed, gate_w, preferred_element_type=jnp.float32) * scale
    up_act = jnp.dot(normed, up_w, preferred_element_type=jnp.float32) * scale
    return row_scale, gate_act, up_act


def flipped(me, flip):
    peer = me
    for bit in range(flip.bit_length()):
        if flip >> bit & 1:
            peer = peer + (1 << bit) - (2 << bit) * ((me // (1 << bit)) % 2)
    return peer


def section_one_rows(x, dy, d_hidden, gate_w, up_w):
    bf16 = jnp.bfloat16
    row_scale, gate_act, up_act = normed_parts(x, gate_w, up_w)
    sigmoid_gate = jax.nn.sigmoid(gate_act)
    hidden = (gate_act * sigmoid_gate * up_act).astype(bf16)
    d_gate = d_hidden * up_act * sigmoid_gate * (1.0 + gate_act * (1.0 - sigmoid_gate))
    d_up = d_hidden * gate_act * sigmoid_gate
    d_normed = (
        contract_last(d_gate.astype(bf16), gate_w) + contract_last(d_up.astype(bf16), up_w)
    ) * x.shape[1] ** (-0.5)
    back = (
        dy
        + row_scale * d_normed
        - x * row_scale**3 * jnp.mean(d_normed * x, axis=1, keepdims=True)
    )
    return hidden, back.astype(bf16)


def keys_kernel(micro_count, routes, partner, *outs):
    me = lax.axis_index("rep")
    for b in range(micro_count):
        outs[b][0] = routes[b, 0] - 1
    outs[micro_count][0] = jnp.bitwise_xor(partner[me], me)


def read_keys(routes, partner):
    in_smem = pl.BlockSpec(memory_space=pltpu.SMEM)
    count = routes.shape[0] + 1
    return pl.pallas_call(
        functools.partial(keys_kernel, routes.shape[0]),
        out_shape=[jax.ShapeDtypeStruct((1,), jnp.int32)] * count,
        in_specs=[in_smem] * 2,
        out_specs=[in_smem] * count,
        name="keys",
    )(routes, partner)


def by_blocks(count, step, stage):
    def run(i, carry):
        stage(pl.ds(pl.multiple_of(i * step, step), step))
        return carry

    lax.fori_loop(0, count // step, run, 0)


def choose(target, flag, left, right):
    def stage(p):
        picked = jnp.where(flag, left[p, :].astype(jnp.float32), right[p, :].astype(jnp.float32))
        target[p, :] = picked.astype(target.dtype)

    by_blocks(target.shape[0], 16 if target.shape[1] > 512 else 64, stage)


def flip_flags(bits):
    return [(bits[0] // (1 << order)) % 2 == 1 for order in range(2)]


SLOW_PIECES = 2


def slow_exchange(me, bits, slow, near, chosen, far, mate, near_send, near_recv, far_send, far_recv):
    size = slow.shape[0] // (2 * SLOW_PIECES)
    peers = (flipped(me, 1), flipped(me, 2))
    flags = flip_flags(bits)

    def place(order, piece):
        return pl.ds((order * SLOW_PIECES + piece) * size, size)

    def near_copy(order, piece):
        p, i = place(order, piece), order * SLOW_PIECES + piece
        return pltpu.make_async_remote_copy(
            src_ref=slow.at[p], dst_ref=near.at[p],
            send_sem=near_send.at[i], recv_sem=near_recv.at[i],
            device_id={"rep": peers[order]}, device_id_type=pl.DeviceIdType.MESH,
        )

    def far_copy(order, piece):
        p, i = place(order, piece), order * SLOW_PIECES + piece
        return pltpu.make_async_remote_copy(
            src_ref=chosen.at[p], dst_ref=far.at[p],
            send_sem=far_send.at[i], recv_sem=far_recv.at[i],
            device_id={"rep": peers[1 - order]}, device_id_type=pl.DeviceIdType.MESH,
        )

    def begin():
        for piece in range(SLOW_PIECES):
            for order in range(2):
                near_copy(order, piece).start()

    def pass_on(piece):
        for order in range(2):
            p = place(order, piece)
            near_copy(order, piece).wait_recv()
            choose(chosen.at[p], flags[order], near.at[p], slow.at[p])
            far_copy(order, piece).start()

    def finish():
        for piece in range(SLOW_PIECES):
            for order in range(2):
                far_copy(order, piece).wait_recv()
        for order in range(2):
            p = pl.ds(order * SLOW_PIECES * size, SLOW_PIECES * size)
            choose(mate.at[p], flags[1 - order], far.at[p], chosen.at[p])
        for piece in range(SLOW_PIECES):
            for order in range(2):
                near_copy(order, piece).wait_send()
                far_copy(order, piece).wait_send()

    return begin, pass_on, finish


def slow_scratch(slow):
    return [pltpu.VMEM(slow.shape, jnp.bfloat16)] * 3


def slow_semaphores():
    return [pltpu.SemaphoreType.DMA((2 * SLOW_PIECES,))] * 4


def greet(me, barrier):
    for flip in (1, 2):
        pl.semaphore_signal(
            barrier, inc=1, device_id={"rep": flipped(me, flip)},
            device_id_type=pl.DeviceIdType.MESH,
        )


def first_kernel(
    flip, chunk, bits, ends, gate_h, up_h, slow_h,
    slow, mate, hidden, dy, next_rows, dh,
    gate, up, sent, x, arrived, near, chosen, far,
    load_sem, row_sem, go_send, go_recv, come_send, come_recv, *slow_sems,
):
    me, section = lax.axis_index("rep"), lax.axis_index("section")
    f32, bf16 = jnp.float32, jnp.bfloat16
    mesh_ids = pl.DeviceIdType.MESH
    rows, _ = dy.shape
    units = slow.shape[0]
    per_batch = rows // chunk
    other = {"rep": flipped(me, flip), "section": 1 - section}
    slow_begin, slow_pass, slow_finish = slow_exchange(
        me, bits, slow, near, chosen, far, mate, *slow_sems
    )

    barrier = pltpu.get_barrier_semaphore()
    pl.semaphore_signal(barrier, inc=1, device_id=other, device_id_type=mesh_ids)

    load_gate, load_up, load_slow = [
        pltpu.make_async_copy(source, target, load_sem.at[i])
        for i, (source, target) in enumerate(((gate_h, gate), (up_h, up), (slow_h, slow)))
    ]
    load_x = pltpu.make_async_copy(ends, x, row_sem)

    @pl.when(section == 1)
    def _():
        greet(me, barrier)
        load_slow.start()

    load_x.start()
    load_gate.start()
    load_up.start()

    @pl.when(section == 0)
    def _():
        load_slow.start()

    def span(c):
        return pl.ds(pl.multiple_of(c * chunk, chunk), chunk)

    def going(c):
        return pltpu.make_async_remote_copy(
            src_ref=sent.at[span(c)], dst_ref=arrived.at[span(c)],
            send_sem=go_send.at[c], recv_sem=go_recv.at[c],
            device_id=other, device_id_type=mesh_ids,
        )

    def coming(c):
        return pltpu.make_async_remote_copy(
            src_ref=sent.at[span(c)], dst_ref=dy.at[span(c)],
            send_sem=come_send.at[c], recv_sem=come_recv.at[c],
            device_id=other, device_id_type=mesh_ids,
        )

    @pl.when(section == 1)
    def _():
        load_slow.wait()
        pl.semaphore_wait(barrier, 3)
        slow_begin()
        load_x.wait()

        def turn_back(b, carry):
            p = pl.ds(pl.multiple_of(b * rows, rows), rows)
            dh[p, :] = contract_last(x[p, :], slow[...]) * units ** (-0.5)
            return carry

        lax.fori_loop(0, 2, turn_back, 0)
        load_gate.wait()
        load_up.wait()
        slow_pass(0)

        def body(c, carry):
            @pl.when(c == per_batch - 1)
            def _():
                for piece in range(1, SLOW_PIECES):
                    slow_pass(piece)

            going(c).wait_recv()
            hid, back = section_one_rows(
                arrived[span(c), :].astype(f32), x[span(c), :].astype(f32), dh[span(c), :],
                gate[...], up[...],
            )
            hidden[span(c), :] = hid
            sent[span(c), :] = back
            coming(c).start()
            return carry

        lax.fori_loop(0, per_batch, body, 0)
        slow_finish()
        for c in range(per_batch):
            coming(c).wait_send()

    @pl.when(section == 0)
    def _():
        load_x.wait()
        load_gate.wait()
        load_up.wait()

        def body(c, carry):
            as_float = x[span(c), :].astype(f32)
            _, gate_act, up_act = normed_parts(as_float, gate[...], up[...])
            hid = (jax.nn.silu(gate_act) * up_act).astype(bf16)
            hidden[span(c), :] = hid

            @pl.when(c == 0)
            def _():
                load_slow.wait()

            branch = jnp.dot(hid, slow[...], preferred_element_type=f32) * units ** (-0.5)
            out_rows = (as_float + branch).astype(bf16)

            @pl.when(c < per_batch)
            def _():
                sent[span(c), :] = out_rows

            @pl.when(c >= per_batch)
            def _():
                next_rows[span(c - per_batch), :] = out_rows

            @pl.when(c == 0)
            def _():
                pl.semaphore_wait(barrier, 1)

            @pl.when(c < per_batch)
            def _():
                going(c).start()

            return carry

        lax.fori_loop(0, 2 * per_batch, body, 0)
        for c in range(per_batch):
            going(c).wait_send()
        for c in range(per_batch):
            coming(c).wait_recv()


def first_trip(flip, chunk, bits, ends, gate_w, up_w, slow):
    model_width, units = gate_w.shape
    rows = ends.shape[0] // 2
    count = rows // chunk
    bf16, f32 = jnp.bfloat16, jnp.float32
    outs = [
        jax.ShapeDtypeStruct(shape, bf16)
        for shape in (slow.shape, slow.shape, (2 * rows, units)) + ((rows, model_width),) * 2
    ] + [jax.ShapeDtypeStruct((2 * rows, units), f32)]
    in_vmem = pl.BlockSpec(memory_space=pltpu.VMEM)
    dma = pltpu.SemaphoreType.DMA
    return pl.pallas_call(
        functools.partial(first_kernel, flip, chunk),
        out_shape=outs,
        in_specs=[pl.BlockSpec(memory_space=pltpu.SMEM)]
        + [pl.BlockSpec(memory_space=pltpu.HBM)] * 4,
        out_specs=[in_vmem] * len(outs),
        scratch_shapes=[
            pltpu.VMEM(gate_w.shape, bf16), pltpu.VMEM(up_w.shape, bf16),
            pltpu.VMEM((rows, model_width), bf16), pltpu.VMEM((2 * rows, model_width), bf16),
            pltpu.VMEM((rows, model_width), bf16),
            *slow_scratch(slow), dma((3,)), dma, *[dma((count,))] * 4, *slow_semaphores(),
        ],
        compiler_params=pltpu.CompilerParams(
            collective_id=flip, has_side_effects=True, vmem_limit_bytes=12 * 1024 * 1024
        ),
        name="first",
    )(bits, ends, gate_w, up_w, slow)


def pseudo_exchange(me, bits, own, near, chosen, far, send_near, recv_near, send_far, recv_far):
    peers = (flipped(me, 1), flipped(me, 2))
    flags = flip_flags(bits)
    f32 = jnp.float32

    def near_copy(c, order):
        return pltpu.make_async_remote_copy(
            src_ref=own.at[c], dst_ref=near.at[c],
            send_sem=send_near.at[c], recv_sem=recv_near.at[c],
            device_id={"rep": peers[order]}, device_id_type=pl.DeviceIdType.MESH,
        )

    def far_copy(c, order):
        return pltpu.make_async_remote_copy(
            src_ref=chosen.at[c], dst_ref=far.at[c],
            send_sem=send_far.at[c], recv_sem=recv_far.at[c],
            device_id={"rep": peers[1 - order]}, device_id_type=pl.DeviceIdType.MESH,
        )

    def pass_on(c, order):
        near_copy(c, order).wait_recv()
        choose(chosen.at[c], flags[order], near.at[c], own.at[c])
        far_copy(c, order).start()

    def mean(c, order, p):
        mate = jnp.where(flags[1 - order], far[c, p, :].astype(f32), chosen[c, p, :].astype(f32))
        return 0.5 * (own[c, p, :].astype(f32) + mate)

    def every(stage):
        def run(pair, carry):
            for order in range(2):
                stage(2 * pair + order, order)
            return carry

        lax.fori_loop(0, own.shape[0] // 2, run, 0)

    return every, near_copy, far_copy, pass_on, mean


def second_kernel(
    flip, chunk, bits, ends, gate_h, up_h, first_in, second_in, momentum,
    slow, mate_in, hidden_in, dy_in, sent, dh,
    new_slow, new_momentum,
    own, mate_slow, gate, up, x, back_rows, hidden, dy, grad, near, chosen, far, near_p, chosen_p, far_p,
    load_sem, row_sem, go_send, go_recv, come_send, come_recv, *sems,
):
    me, section = lax.axis_index("rep"), lax.axis_index("section")
    f32, bf16 = jnp.float32, jnp.bfloat16
    mesh_ids = pl.DeviceIdType.MESH
    rows, model_width = x.shape
    units, width = own.shape[1:]
    count = rows // chunk
    other = {"rep": flipped(me, flip), "section": 1 - section}
    slow_begin, slow_pass, slow_finish = slow_exchange(
        me, bits, slow, near, chosen, far, mate_slow, *sems[:4]
    )
    every, near_copy, far_copy, pass_on, mean_of = pseudo_exchange(
        me, bits, own, near_p, chosen_p, far_p, *sems[4:]
    )

    barrier = pltpu.get_barrier_semaphore()
    pl.semaphore_signal(barrier, inc=1, device_id=other, device_id_type=mesh_ids)
    greet(me, barrier)
    load_gate = pltpu.make_async_copy(gate_h, gate, load_sem.at[0])
    load_up = pltpu.make_async_copy(up_h, up, load_sem.at[1])
    load_dy = pltpu.make_async_copy(ends, dy, row_sem)

    def span(c, base=0):
        return pl.ds(pl.multiple_of(base + c * chunk, chunk), chunk)

    def going(c):
        return pltpu.make_async_remote_copy(
            src_ref=sent.at[span(c)], dst_ref=x.at[span(c)],
            send_sem=go_send.at[c], recv_sem=go_recv.at[c],
            device_id=other, device_id_type=mesh_ids,
        )

    def coming(c):
        return pltpu.make_async_remote_copy(
            src_ref=back_rows.at[span(c)], dst_ref=dy.at[span(c, rows)],
            send_sem=come_send.at[c], recv_sem=come_recv.at[c],
            device_id=other, device_id_type=mesh_ids,
        )

    @pl.when(section == 1)
    def _():
        load_dy.start()
        load_gate.start()
        load_up.start()

    pl.semaphore_wait(barrier, 3)

    @pl.when(section == 0)
    def _():
        for c in range(count):
            going(c).start()
        slow_begin()

    def keep(source, target):
        def stage(p):
            target[p, :] = source[p, :]

        by_blocks(source.shape[0], 16, stage)

    keep(hidden_in, hidden)

    @pl.when(section == 1)
    def _():
        keep(mate_in, mate_slow)
        load_dy.wait()
        load_gate.wait()
        load_up.wait()

        def body(c, carry):
            going(c).wait_recv()
            hid, back = section_one_rows(
                x[span(c), :].astype(f32), dy[span(c, rows), :].astype(f32),
                dh[span(c, rows), :],
                gate[...], up[...],
            )
            hidden[span(c, rows), :] = hid
            back_rows[span(c), :] = back
            coming(c).start()
            return carry

        lax.fori_loop(0, count, body, 0)

    @pl.when(section == 0)
    def _():
        keep(dy_in, dy)
        for piece in range(SLOW_PIECES):
            slow_pass(piece)
        slow_finish()
        for c in range(count):
            going(c).wait_send()
        for c in range(count):
            coming(c).wait_recv()

    wide = grad.shape[1]

    def begin(part, pair, order):
        c = part * (wide // width) + 2 * pair + order
        p = pl.ds(pl.multiple_of(c * width, width), width)
        local = pl.ds(pl.multiple_of((2 * pair + order) * width, width), width)

        def stage(q):
            g = grad[q, local]
            first = 0.9 * first_in[q, p].astype(f32) + 0.1 * g
            second = 0.999 * second_in[q, p].astype(f32) + 0.001 * g * g
            step = first / (jnp.sqrt(second) + 1e-08)
            own[c, q, :] = (step + 0.1 * slow[q, p].astype(f32)).astype(bf16)

        by_blocks(units, 128, stage)
        near_copy(c, order).start()

    def finish(c, order):
        p = pl.ds(pl.multiple_of(c * width, width), width)
        far_copy(c, order).wait_recv()

        def stage(q):
            mean = mean_of(c, order, q)
            moment = 0.9 * momentum[q, p].astype(f32) + mean
            averaged = 0.5 * (slow[q, p].astype(f32) + mate_slow[q, p].astype(f32))
            new_slow[q, p] = (averaged - 0.014 * (0.9 * moment + mean)).astype(bf16)
            new_momentum[q, p] = moment.astype(bf16)

        by_blocks(units, 128, stage)
        near_copy(c, order).wait_send()
        far_copy(c, order).wait_send()

    def run_part(part, carry):
        columns = pl.ds(pl.multiple_of(part * wide, wide), wide)
        grad[...] = grad_rows(dy[:, columns], hidden[...], units)

        def run_pair(pair, carry):
            for order in range(2):
                begin(part, pair, order)
            return carry

        return lax.fori_loop(0, wide // (2 * width), run_pair, carry)

    lax.fori_loop(0, model_width // wide, run_part, 0)
    every(pass_on)
    every(finish)

    @pl.when(section == 1)
    def _():
        for c in range(count):
            coming(c).wait_send()


def second_trip(
    flip, chunk, bits, ends, gate_w, up_w, first_in, second_in, momentum,
    slow, mate, hidden, dy, sent, dh,
):
    model_width, units = gate_w.shape
    rows = ends.shape[0] // 2
    count = rows // chunk
    width = 128
    chunks = model_width // width
    bf16, f32 = jnp.bfloat16, jnp.float32
    block = (chunks, units, width)
    outs = [jax.ShapeDtypeStruct(slow.shape, bf16)] * 2
    in_vmem = pl.BlockSpec(memory_space=pltpu.VMEM)
    dma = pltpu.SemaphoreType.DMA
    return pl.pallas_call(
        functools.partial(second_kernel, flip, chunk),
        out_shape=outs,
        in_specs=[pl.BlockSpec(memory_space=pltpu.SMEM)]
        + [pl.BlockSpec(memory_space=pltpu.HBM)] * 3
        + [in_vmem] * 9,
        out_specs=[in_vmem] * len(outs),
        scratch_shapes=[
            pltpu.VMEM(block, bf16), pltpu.VMEM(slow.shape, bf16),
            pltpu.VMEM(gate_w.shape, bf16), pltpu.VMEM(up_w.shape, bf16),
            pltpu.VMEM((rows, model_width), bf16), pltpu.VMEM((rows, model_width), bf16),
            pltpu.VMEM((2 * rows, units), bf16), pltpu.VMEM((2 * rows, model_width), bf16),
            pltpu.VMEM((units, model_width // 2), f32),
            *slow_scratch(slow), *[pltpu.VMEM(block, bf16)] * 3,
            dma((2,)), dma, *[dma((count,))] * 4, *slow_semaphores(), *[dma((chunks,))] * 4,
        ],
        compiler_params=pltpu.CompilerParams(
            collective_id=16 + flip, has_side_effects=True, vmem_limit_bytes=12 * 1024 * 1024
        ),
        name="second",
    )(
        bits, ends, gate_w, up_w, first_in, second_in, momentum,
        slow, mate, hidden, dy, sent, dh,
    )


def last_kernel(new_slow, new_momentum, new_slow_h, new_momentum_h, sems):
    puts = (
        pltpu.make_async_copy(new_slow, new_slow_h, sems.at[0]),
        pltpu.make_async_copy(new_momentum, new_momentum_h, sems.at[1]),
    )
    for put in puts:
        put.start()
    for put in puts:
        put.wait()


def last_step(new_slow, new_momentum):
    out = jax.ShapeDtypeStruct(new_slow.shape, jnp.bfloat16)
    in_vmem = pl.BlockSpec(memory_space=pltpu.VMEM)
    in_hbm = pl.BlockSpec(memory_space=pltpu.HBM)
    return pl.pallas_call(
        last_kernel,
        out_shape=(out, out),
        in_specs=[in_vmem] * 2,
        out_specs=(in_hbm, in_hbm),
        scratch_shapes=[pltpu.SemaphoreType.DMA((2,))],
        compiler_params=pltpu.CompilerParams(vmem_limit_bytes=8 * 1024 * 1024),
        name="last",
    )(new_slow, new_momentum)


def trip_on_device(ends, w_gate, w_up, slow_down, adam_m, adam_v, momentum, routes, partner):
    micro_count, row_count, model_width = ends.shape[2:]
    flat_ends = ends.reshape(micro_count * row_count, model_width)
    gate_w, up_w, down_w = w_gate[0, 0], w_up[0, 0], slow_down[0, 0]
    chunk = row_count // 2
    flips = range(1, lax.axis_size("rep"))
    *keys, bits = read_keys(routes, partner)
    slow_v, mate_slow, hidden, dy, sent, dh = lax.switch(
        keys[0][0],
        [functools.partial(first_trip, flip, chunk) for flip in flips],
        bits, flat_ends, gate_w, up_w, down_w,
    )
    new_slow, new_momentum = lax.switch(
        keys[1][0],
        [functools.partial(second_trip, flip, chunk) for flip in flips],
        bits, flat_ends, gate_w, up_w, adam_m[0, 0], adam_v[0, 0], momentum[0, 0],
        slow_v, mate_slow, hidden, dy, sent, dh,
    )
    new_slow, new_momentum = last_step(new_slow, new_momentum)
    return new_slow[None, None], new_momentum[None, None]


def wide_on_device(ends, w_gate, w_up, slow_down, adam_m, adam_v, momentum, routes, partner):
    micro_count, row_count, model_width = ends.shape[2:]
    own_data = ends.reshape(micro_count * row_count, model_width)
    gate_w = w_gate[0, 0]
    up_w = w_up[0, 0]
    down_w = slow_down[0, 0]
    hidden_units = gate_w.shape[1]
    replica = lax.axis_index("rep")
    on_first = lax.axis_index("section") == 0
    flip_keys = routes[:, 0]
    flip_bits = jnp.bitwise_xor(partner[replica], replica)
    near_slow = partner_2(down_w, "rep", 0)

    def cut(rows):
        return rows.reshape(micro_count, row_count, model_width)

    def first_forward():
        result, saved = forward_rows(own_data, gate_w, up_w, down_w)
        return result, saved[3]

    def first_idle():
        return own_data, jnp.zeros((own_data.shape[0], hidden_units), jnp.bfloat16)

    sent, hidden = lax.cond(on_first, first_forward, first_idle)
    sent = cut(sent)
    arrived = [send_rows(sent[b], flip_keys[b], 0) for b in range(micro_count)]
    near_slow, *arrived = lax.optimization_barrier((near_slow, *arrived))
    arrived = jnp.concatenate(arrived)
    chosen_slow = jnp.where(flip_bits & 1 == 1, near_slow, down_w)
    far_slow = partner_2(chosen_slow, "rep", 1)

    def last_work():
        _, saved = forward_rows(arrived, gate_w, up_w, down_w)
        term, back = backward_rows(own_data, arrived, saved, gate_w, up_w, down_w)
        return term, back

    def last_idle():
        return jnp.zeros((hidden_units, model_width), jnp.float32), own_data

    last_term, back = lax.cond(on_first, last_idle, last_work)
    back = cut(back)
    returned = [send_rows(back[b], flip_keys[b], 1) for b in range(micro_count)]
    far_slow, *returned = lax.optimization_barrier((far_slow, *returned))
    returned = jnp.concatenate(returned)
    partner_slow = jnp.where(flip_bits >> 1 & 1 == 1, far_slow, chosen_slow)
    grad_sum = lax.cond(
        on_first, lambda: grad_rows(returned, hidden, hidden_units), lambda: last_term
    )
    masks = jnp.zeros((8, model_width), jnp.int32)
    masks = masks.at[0].set(flip_bits & 1).at[1].set(flip_bits >> 1 & 1)
    new_slow, new_momentum = outer_update(
        masks, grad_sum, adam_m[0, 0], adam_v[0, 0], down_w, partner_slow, momentum[0, 0]
    )
    return new_slow[None, None], new_momentum[None, None]


def solution(mesh):
    weights = P("section", "rep", None, None)
    placed = (P("section", "rep", None, None, None),) + (weights,) * 6 + (P(), P())
    narrow = mesh.shape["rep"] <= 16
    on_device = trip_on_device if narrow else wide_on_device

    return jax.shard_map(
        on_device, mesh=mesh, in_specs=placed, out_specs=(weights, weights), check_vma=False
    )
```

```python
import functools

import jax
import jax.numpy as jnp
from jax import lax
from jax.experimental import pallas as pl
from jax.experimental.pallas import tpu as pltpu
from jax.sharding import PartitionSpec as P


def partner_2(x, axis, bit):
    return lax.ppermute(x, axis, [(i, i ^ 1 << bit) for i in range(lax.axis_size(axis))])


def forward_rows(in_rows, w_gate, w_up, w_down):
    model_width = in_rows.shape[1]
    hidden_units = w_gate.shape[1]
    as_float = in_rows.astype(jnp.float32)
    row_scale = lax.rsqrt(jnp.mean(as_float * as_float, axis=1, keepdims=True) + 1e-06)
    normed = (as_float * row_scale).astype(jnp.bfloat16)
    gate_act = jnp.dot(normed, w_gate, preferred_element_type=jnp.float32) * model_width ** (-0.5)
    up_act = jnp.dot(normed, w_up, preferred_element_type=jnp.float32) * model_width ** (-0.5)
    hidden = (jax.nn.silu(gate_act) * up_act).astype(jnp.bfloat16)
    branch = jnp.dot(hidden, w_down, preferred_element_type=jnp.float32) * hidden_units ** (-0.5)
    result = (as_float + branch).astype(jnp.bfloat16)
    return (result, (row_scale, gate_act, up_act, hidden))


def contract_last(left, right):
    return lax.dot_general(
        left, right, (((1,), (1,)), ((), ())), preferred_element_type=jnp.float32
    )


def grad_rows(cotangent, hidden, hidden_units):
    return lax.dot_general(
        hidden, cotangent, (((0,), (0,)), ((), ())), preferred_element_type=jnp.float32
    ) * hidden_units ** (-0.5)


def backward_rows(cotangent, in_rows, saved_state, w_gate, w_up, w_down):
    row_scale, gate_act, up_act, hidden = saved_state
    model_width = in_rows.shape[1]
    hidden_units = w_gate.shape[1]
    d_hidden = contract_last(cotangent, w_down) * hidden_units ** (-0.5)
    grad_term = grad_rows(cotangent, hidden, hidden_units)
    sigmoid_gate = jax.nn.sigmoid(gate_act)
    d_gate = (d_hidden * up_act * sigmoid_gate * (1.0 + gate_act * (1.0 - sigmoid_gate))).astype(
        jnp.bfloat16
    )
    d_up = (d_hidden * gate_act * sigmoid_gate).astype(jnp.bfloat16)
    d_normed = (contract_last(d_gate, w_gate) + contract_last(d_up, w_up)) * model_width ** (-0.5)
    as_float = in_rows.astype(jnp.float32)
    back_rows = (
        cotangent.astype(jnp.float32)
        + row_scale * d_normed
        - as_float * row_scale**3 * jnp.mean(d_normed * as_float, axis=1, keepdims=True)
    )
    return (grad_term, back_rows.astype(jnp.bfloat16))


def hop_kernel(flip, source, target, rows, out, send_sem, recv_sem):
    me, section = lax.axis_index("rep"), lax.axis_index("section")
    peer = me
    for bit in range(flip.bit_length()):
        if flip >> bit & 1:
            peer = peer + (1 << bit) - (2 << bit) * ((me // (1 << bit)) % 2)
    other = {"rep": peer, "section": section if source == target else 1 - section}
    barrier = pltpu.get_barrier_semaphore()
    pl.semaphore_signal(barrier, inc=1, device_id=other, device_id_type=pl.DeviceIdType.MESH)
    pl.semaphore_wait(barrier, 1)
    copy = pltpu.make_async_remote_copy(
        src_ref=rows, dst_ref=out, send_sem=send_sem, recv_sem=recv_sem,
        device_id=other, device_id_type=pl.DeviceIdType.MESH,
    )

    @pl.when(section == source)
    def _():
        copy.start()
        copy.wait_send()

    @pl.when(section == target)
    def _():
        copy.wait_recv()


def send_rows(payload, flip_key, source):
    bits = lax.axis_size("rep").bit_length() - 1
    starts = list(range(0, bits, 4))
    for index, start in enumerate(starts):
        width = min(4, bits - start)
        target = 1 - source if start == starts[-1] else source

        def branch(flip, index=index, start=start, target=target):
            if target == source and flip == 0:
                return lambda rows: rows
            in_vmem = pl.BlockSpec(memory_space=pltpu.VMEM)
            return pl.pallas_call(
                functools.partial(hop_kernel, flip << start, source, target),
                out_shape=jax.ShapeDtypeStruct(payload.shape, payload.dtype),
                in_specs=[in_vmem],
                out_specs=in_vmem,
                scratch_shapes=[pltpu.SemaphoreType.DMA, pltpu.SemaphoreType.DMA],
                compiler_params=pltpu.CompilerParams(
                    collective_id=1 + (index * 2 + source) * 16 + flip,
                    has_side_effects=True,
                    vmem_limit_bytes=4 * 1024 * 1024,
                ),
                name="hop",
            )

        payload = lax.switch(
            flip_key >> start & (1 << width) - 1, [branch(f) for f in range(1 << width)], payload
        )
    return payload


def outer_kernel(
    chunks, masks, grad, first_in, second_in, slow, mate_slow, momentum,
    new_slow, new_momentum, own, near, chosen, far, send_near, recv_near, send_far, recv_far,
):
    me = lax.axis_index("rep")
    peers = (me + 1 - 2 * (me % 2), me + 2 - 4 * ((me // 2) % 2))
    rows = grad.shape[0] // chunks
    f32, bf16 = jnp.float32, jnp.bfloat16

    barrier = pltpu.get_barrier_semaphore()
    for peer in peers:
        pl.semaphore_signal(
            barrier, inc=1, device_id={"rep": peer}, device_id_type=pl.DeviceIdType.MESH
        )

    def part(c):
        return pl.ds(pl.multiple_of(c * rows, rows), rows)

    def near_copy(c, order):
        return pltpu.make_async_remote_copy(
            src_ref=own.at[part(c)], dst_ref=near.at[part(c)],
            send_sem=send_near.at[c], recv_sem=recv_near.at[c],
            device_id={"rep": peers[order]}, device_id_type=pl.DeviceIdType.MESH,
        )

    def far_copy(c, order):
        return pltpu.make_async_remote_copy(
            src_ref=chosen.at[part(c)], dst_ref=far.at[part(c)],
            send_sem=send_far.at[c], recv_sem=recv_far.at[c],
            device_id={"rep": peers[1 - order]}, device_id_type=pl.DeviceIdType.MESH,
        )

    def adam(c):
        p = part(c)
        g = grad[p, :]
        first = 0.9 * first_in[p, :].astype(f32) + 0.1 * g
        second = 0.999 * second_in[p, :].astype(f32) + 0.001 * g * g
        step = first / (jnp.sqrt(second) + 1e-08)
        own[p, :] = (step + 0.1 * slow[p, :].astype(f32)).astype(bf16)

    def send(c, order):
        near_copy(c, order).start()

    def begin(c, order):
        adam(c)
        send(c, order)

    def pass_on(c, order):
        p = part(c)
        near_copy(c, order).wait_recv()
        chosen[p, :] = jnp.where(
            masks[order : order + 1, :] == 1, near[p, :].astype(f32), own[p, :].astype(f32)
        ).astype(bf16)
        far_copy(c, order).start()

    def finish(c, order):
        p = part(c)
        far_copy(c, order).wait_recv()
        mate = jnp.where(
            masks[1 - order : 2 - order, :] == 1, far[p, :].astype(f32), chosen[p, :].astype(f32)
        )
        mean = 0.5 * (own[p, :].astype(f32) + mate)
        moment = 0.9 * momentum[p, :].astype(f32) + mean
        averaged = 0.5 * (slow[p, :].astype(f32) + mate_slow[p, :].astype(f32))
        new_slow[p, :] = (averaged - 0.014 * (0.9 * moment + mean)).astype(bf16)
        new_momentum[p, :] = moment.astype(bf16)

    def settle(c, order):
        near_copy(c, order).wait_send()
        far_copy(c, order).wait_send()

    def both(start, stop, *stages):
        def run(pair, carry):
            for stage in stages:
                for order in range(2):
                    stage(2 * pair + order, order)
            return carry

        lax.fori_loop(start, stop, run, 0)

    pairs = chunks // 2
    both(0, 1, lambda c, order: adam(c))
    pl.semaphore_wait(barrier, 2)
    both(0, 1, send)
    both(1, pairs, begin)
    both(0, 1, pass_on)
    both(1, pairs, pass_on, lambda c, order: finish(c - 2, order))
    both(pairs - 1, pairs, finish)
    both(0, pairs, settle)


def outer_update(masks, grad, first_in, second_in, slow, mate_slow, momentum):
    hidden_units, model_width = grad.shape
    chunks = hidden_units // 32
    block = pltpu.VMEM((hidden_units, model_width), jnp.bfloat16)
    sems = pltpu.SemaphoreType.DMA((chunks,))
    out = jax.ShapeDtypeStruct((hidden_units, model_width), jnp.bfloat16)
    in_vmem = pl.BlockSpec(memory_space=pltpu.VMEM)
    return pl.pallas_call(
        functools.partial(outer_kernel, chunks),
        out_shape=(out, out),
        in_specs=[in_vmem] * 7,
        out_specs=(in_vmem, in_vmem),
        scratch_shapes=[block] * 4 + [sems] * 4,
        compiler_params=pltpu.CompilerParams(
            collective_id=0, has_side_effects=True, vmem_limit_bytes=16 * 1024 * 1024
        ),
        name="outer",
    )(masks, grad, first_in, second_in, slow, mate_slow, momentum)


def normed_parts(x, gate_w, up_w):
    model_width = x.shape[1]
    row_scale = lax.rsqrt(jnp.mean(x * x, axis=1, keepdims=True) + 1e-06)
    normed = (x * row_scale).astype(jnp.bfloat16)
    scale = model_width ** (-0.5)
    gate_act = jnp.dot(normed, gate_w, preferred_element_type=jnp.float32) * scale
    up_act = jnp.dot(normed, up_w, preferred_element_type=jnp.float32) * scale
    return row_scale, gate_act, up_act


def flipped(me, flip):
    peer = me
    for bit in range(flip.bit_length()):
        if flip >> bit & 1:
            peer = peer + (1 << bit) - (2 << bit) * ((me // (1 << bit)) % 2)
    return peer


def section_one_rows(x, dy, d_hidden, gate_w, up_w):
    bf16 = jnp.bfloat16
    row_scale, gate_act, up_act = normed_parts(x, gate_w, up_w)
    sigmoid_gate = jax.nn.sigmoid(gate_act)
    hidden = (gate_act * sigmoid_gate * up_act).astype(bf16)
    d_gate = d_hidden * up_act * sigmoid_gate * (1.0 + gate_act * (1.0 - sigmoid_gate))
    d_up = d_hidden * gate_act * sigmoid_gate
    d_normed = (
        contract_last(d_gate.astype(bf16), gate_w) + contract_last(d_up.astype(bf16), up_w)
    ) * x.shape[1] ** (-0.5)
    back = (
        dy
        + row_scale * d_normed
        - x * row_scale**3 * jnp.mean(d_normed * x, axis=1, keepdims=True)
    )
    return hidden, back.astype(bf16)


def keys_kernel(micro_count, routes, partner, *outs):
    me = lax.axis_index("rep")
    for b in range(micro_count):
        outs[b][0] = routes[b, 0] - 1
    outs[micro_count][0] = jnp.bitwise_xor(partner[me], me)


def read_keys(routes, partner):
    in_smem = pl.BlockSpec(memory_space=pltpu.SMEM)
    count = routes.shape[0] + 1
    return pl.pallas_call(
        functools.partial(keys_kernel, routes.shape[0]),
        out_shape=[jax.ShapeDtypeStruct((1,), jnp.int32)] * count,
        in_specs=[in_smem] * 2,
        out_specs=[in_smem] * count,
        name="keys",
    )(routes, partner)


def by_blocks(count, step, stage):
    def run(i, carry):
        stage(pl.ds(pl.multiple_of(i * step, step), step))
        return carry

    lax.fori_loop(0, count // step, run, 0)


def choose(target, flag, left, right):
    def stage(p):
        picked = jnp.where(flag, left[p, :].astype(jnp.float32), right[p, :].astype(jnp.float32))
        target[p, :] = picked.astype(target.dtype)

    by_blocks(target.shape[0], 16 if target.shape[1] > 512 else 64, stage)


def flip_flags(bits):
    return [(bits[0] // (1 << order)) % 2 == 1 for order in range(2)]


SLOW_PIECES = 2


def slow_exchange(me, bits, slow, near, chosen, far, mate, near_send, near_recv, far_send, far_recv):
    size = slow.shape[0] // (2 * SLOW_PIECES)
    peers = (flipped(me, 1), flipped(me, 2))
    flags = flip_flags(bits)

    def place(order, piece):
        return pl.ds((order * SLOW_PIECES + piece) * size, size)

    def near_copy(order, piece):
        p, i = place(order, piece), order * SLOW_PIECES + piece
        return pltpu.make_async_remote_copy(
            src_ref=slow.at[p], dst_ref=near.at[p],
            send_sem=near_send.at[i], recv_sem=near_recv.at[i],
            device_id={"rep": peers[order]}, device_id_type=pl.DeviceIdType.MESH,
        )

    def far_copy(order, piece):
        p, i = place(order, piece), order * SLOW_PIECES + piece
        return pltpu.make_async_remote_copy(
            src_ref=chosen.at[p], dst_ref=far.at[p],
            send_sem=far_send.at[i], recv_sem=far_recv.at[i],
            device_id={"rep": peers[1 - order]}, device_id_type=pl.DeviceIdType.MESH,
        )

    def begin():
        for piece in range(SLOW_PIECES):
            for order in range(2):
                near_copy(order, piece).start()

    def pass_on(piece):
        for order in range(2):
            p = place(order, piece)
            near_copy(order, piece).wait_recv()
            choose(chosen.at[p], flags[order], near.at[p], slow.at[p])
            far_copy(order, piece).start()

    def finish():
        for piece in range(SLOW_PIECES):
            for order in range(2):
                far_copy(order, piece).wait_recv()
        for order in range(2):
            p = pl.ds(order * SLOW_PIECES * size, SLOW_PIECES * size)
            choose(mate.at[p], flags[1 - order], far.at[p], chosen.at[p])
        for piece in range(SLOW_PIECES):
            for order in range(2):
                near_copy(order, piece).wait_send()
                far_copy(order, piece).wait_send()

    return begin, pass_on, finish


def slow_scratch(slow):
    return [pltpu.VMEM(slow.shape, jnp.bfloat16)] * 3


def slow_semaphores():
    return [pltpu.SemaphoreType.DMA((2 * SLOW_PIECES,))] * 4


def greet(me, barrier):
    for flip in (1, 2):
        pl.semaphore_signal(
            barrier, inc=1, device_id={"rep": flipped(me, flip)},
            device_id_type=pl.DeviceIdType.MESH,
        )


def first_kernel(
    flip, chunk, bits, ends, gate_h, up_h, slow_h, first_h, second_h, momentum_h,
    slow, mate, hidden, dy, next_rows, next_dh,
    gate, up, sent, x, arrived, dh, near, chosen, far,
    load_sem, row_sem, go_send, go_recv, come_send, come_recv, *slow_sems,
):
    me, section = lax.axis_index("rep"), lax.axis_index("section")
    f32, bf16 = jnp.float32, jnp.bfloat16
    mesh_ids = pl.DeviceIdType.MESH
    rows, _ = dy.shape
    units = slow.shape[0]
    per_batch = rows // chunk
    other = {"rep": flipped(me, flip), "section": 1 - section}
    slow_begin, slow_pass, slow_finish = slow_exchange(
        me, bits, slow, near, chosen, far, mate, *slow_sems
    )

    barrier = pltpu.get_barrier_semaphore()
    pl.semaphore_signal(barrier, inc=1, device_id=other, device_id_type=mesh_ids)

    load_gate, load_up, load_slow = [
        pltpu.make_async_copy(source, target, load_sem.at[i])
        for i, (source, target) in enumerate(((gate_h, gate), (up_h, up), (slow_h, slow)))
    ]
    load_x = pltpu.make_async_copy(ends, x, row_sem)

    @pl.when(section == 1)
    def _():
        greet(me, barrier)
        load_slow.start()

    load_x.start()
    load_gate.start()
    load_up.start()

    @pl.when(section == 0)
    def _():
        load_slow.start()

    def span(c):
        return pl.ds(pl.multiple_of(c * chunk, chunk), chunk)

    def going(c):
        return pltpu.make_async_remote_copy(
            src_ref=sent.at[span(c)], dst_ref=arrived.at[span(c)],
            send_sem=go_send.at[c], recv_sem=go_recv.at[c],
            device_id=other, device_id_type=mesh_ids,
        )

    def coming(c):
        return pltpu.make_async_remote_copy(
            src_ref=sent.at[span(c)], dst_ref=dy.at[span(c)],
            send_sem=come_send.at[c], recv_sem=come_recv.at[c],
            device_id=other, device_id_type=mesh_ids,
        )

    @pl.when(section == 1)
    def _():
        load_slow.wait()
        pl.semaphore_wait(barrier, 3)
        slow_begin()
        load_x.wait()

        def turn_back(b, carry):
            p = pl.ds(pl.multiple_of(b * rows, rows), rows)
            dh[p, :] = contract_last(x[p, :], slow[...]) * units ** (-0.5)
            return carry

        lax.fori_loop(0, 2, turn_back, 0)

        def hand_on(p):
            next_dh[p, :] = dh[pl.ds(pl.multiple_of(rows + p.start, 16), 16), :]

        by_blocks(rows, 16, hand_on)
        load_gate.wait()
        load_up.wait()

        def body(c, carry):
            @pl.when(c == per_batch - 1)
            def _():
                slow_pass(0)

            going(c).wait_recv()
            hid, back = section_one_rows(
                arrived[span(c), :].astype(f32), x[span(c), :].astype(f32), dh[span(c), :],
                gate[...], up[...],
            )
            hidden[span(c), :] = hid
            sent[span(c), :] = back
            coming(c).start()
            return carry

        lax.fori_loop(0, per_batch, body, 0)
        for piece in range(1, SLOW_PIECES):
            slow_pass(piece)
        slow_finish()
        for c in range(per_batch):
            coming(c).wait_send()

    @pl.when(section == 0)
    def _():
        load_x.wait()
        load_gate.wait()
        load_up.wait()

        def body(c, carry):
            as_float = x[span(c), :].astype(f32)
            _, gate_act, up_act = normed_parts(as_float, gate[...], up[...])
            hid = (jax.nn.silu(gate_act) * up_act).astype(bf16)
            hidden[span(c), :] = hid

            @pl.when(c == 0)
            def _():
                load_slow.wait()

            branch = jnp.dot(hid, slow[...], preferred_element_type=f32) * units ** (-0.5)
            out_rows = (as_float + branch).astype(bf16)

            @pl.when(c < per_batch)
            def _():
                sent[span(c), :] = out_rows

            @pl.when(c >= per_batch)
            def _():
                next_rows[span(c - per_batch), :] = out_rows

            @pl.when(c == 0)
            def _():
                pl.semaphore_wait(barrier, 1)

            @pl.when(c < per_batch)
            def _():
                going(c).start()

            return carry

        lax.fori_loop(0, 2 * per_batch, body, 0)
        for c in range(per_batch):
            going(c).wait_send()
        for c in range(per_batch):
            coming(c).wait_recv()


def first_trip(flip, chunk, bits, ends, gate_w, up_w, slow, *states):
    model_width, units = gate_w.shape
    rows = ends.shape[0] // 2
    count = rows // chunk
    bf16, f32 = jnp.bfloat16, jnp.float32
    outs = [
        jax.ShapeDtypeStruct(shape, bf16)
        for shape in (slow.shape, slow.shape, (2 * rows, units)) + ((rows, model_width),) * 2
    ] + [jax.ShapeDtypeStruct((rows, units), f32)]
    in_vmem = pl.BlockSpec(memory_space=pltpu.VMEM)
    dma = pltpu.SemaphoreType.DMA
    return pl.pallas_call(
        functools.partial(first_kernel, flip, chunk),
        out_shape=outs,
        in_specs=[pl.BlockSpec(memory_space=pltpu.SMEM)]
        + [pl.BlockSpec(memory_space=pltpu.HBM)] * (4 + len(states)),
        out_specs=[in_vmem] * len(outs),
        scratch_shapes=[
            pltpu.VMEM(gate_w.shape, bf16), pltpu.VMEM(up_w.shape, bf16),
            pltpu.VMEM((rows, model_width), bf16), pltpu.VMEM((2 * rows, model_width), bf16),
            pltpu.VMEM((rows, model_width), bf16), pltpu.VMEM((2 * rows, units), f32),
            *slow_scratch(slow), dma((3,)), dma, *[dma((count,))] * 4, *slow_semaphores(),
        ],
        compiler_params=pltpu.CompilerParams(
            collective_id=flip, has_side_effects=True, vmem_limit_bytes=14 * 1024 * 1024
        ),
        name="first",
    )(bits, ends, gate_w, up_w, slow, *states)


def pseudo_exchange(me, bits, own, near, chosen, far, send_near, recv_near, send_far, recv_far):
    peers = (flipped(me, 1), flipped(me, 2))
    flags = flip_flags(bits)
    f32 = jnp.float32

    def near_copy(c, order):
        return pltpu.make_async_remote_copy(
            src_ref=own.at[c], dst_ref=near.at[c],
            send_sem=send_near.at[c], recv_sem=recv_near.at[c],
            device_id={"rep": peers[order]}, device_id_type=pl.DeviceIdType.MESH,
        )

    def far_copy(c, order):
        return pltpu.make_async_remote_copy(
            src_ref=chosen.at[c], dst_ref=far.at[c],
            send_sem=send_far.at[c], recv_sem=recv_far.at[c],
            device_id={"rep": peers[1 - order]}, device_id_type=pl.DeviceIdType.MESH,
        )

    def pass_on(c, order):
        near_copy(c, order).wait_recv()
        choose(chosen.at[c], flags[order], near.at[c], own.at[c])
        far_copy(c, order).start()

    def mean(c, order, p):
        mate = jnp.where(flags[1 - order], far[c, p, :].astype(f32), chosen[c, p, :].astype(f32))
        return 0.5 * (own[c, p, :].astype(f32) + mate)

    def every(stage):
        def run(pair, carry):
            for order in range(2):
                stage(2 * pair + order, order)
            return carry

        lax.fori_loop(0, own.shape[0] // 2, run, 0)

    return every, near_copy, far_copy, pass_on, mean


def second_kernel(
    flip, chunk, bits, ends, gate_h, up_h, first_h, second_h, momentum_h,
    slow, mate_in, hidden_in, dy_in, sent, dh,
    new_slow, new_momentum,
    own, mate_slow, gate, up, first_in, second_in, momentum, x, back_rows, hidden, dy, grad, near, chosen, far, near_p, chosen_p, far_p,
    load_sem, row_sem, go_send, go_recv, come_send, come_recv, *sems,
):
    me, section = lax.axis_index("rep"), lax.axis_index("section")
    f32, bf16 = jnp.float32, jnp.bfloat16
    mesh_ids = pl.DeviceIdType.MESH
    rows, model_width = x.shape
    units, width = own.shape[1:]
    count = rows // chunk
    other = {"rep": flipped(me, flip), "section": 1 - section}
    slow_begin, slow_pass, slow_finish = slow_exchange(
        me, bits, slow, near, chosen, far, mate_slow, *sems[:4]
    )
    every, near_copy, far_copy, pass_on, mean_of = pseudo_exchange(
        me, bits, own, near_p, chosen_p, far_p, *sems[4:]
    )

    barrier = pltpu.get_barrier_semaphore()
    pl.semaphore_signal(barrier, inc=1, device_id=other, device_id_type=mesh_ids)
    greet(me, barrier)
    load_gate = pltpu.make_async_copy(gate_h, gate, load_sem.at[0])
    load_up = pltpu.make_async_copy(up_h, up, load_sem.at[1])
    load_states = [
        pltpu.make_async_copy(source, target, load_sem.at[2 + i])
        for i, (source, target) in enumerate(
            ((first_h, first_in), (second_h, second_in), (momentum_h, momentum))
        )
    ]
    load_dy = pltpu.make_async_copy(ends, dy, row_sem)

    def span(c, base=0):
        return pl.ds(pl.multiple_of(base + c * chunk, chunk), chunk)

    def going(c):
        return pltpu.make_async_remote_copy(
            src_ref=sent.at[span(c)], dst_ref=x.at[span(c)],
            send_sem=go_send.at[c], recv_sem=go_recv.at[c],
            device_id=other, device_id_type=mesh_ids,
        )

    def coming(c):
        return pltpu.make_async_remote_copy(
            src_ref=back_rows.at[span(c)], dst_ref=dy.at[span(c, rows)],
            send_sem=come_send.at[c], recv_sem=come_recv.at[c],
            device_id=other, device_id_type=mesh_ids,
        )

    @pl.when(section == 1)
    def _():
        load_dy.start()
        load_gate.start()
        load_up.start()

    pl.semaphore_wait(barrier, 3)

    @pl.when(section == 0)
    def _():
        for c in range(count):
            going(c).start()
        slow_begin()

    def keep(source, target):
        def stage(p):
            target[p, :] = source[p, :]

        by_blocks(source.shape[0], 16, stage)

    for load in load_states:
        load.start()
    keep(hidden_in, hidden)

    @pl.when(section == 1)
    def _():
        keep(mate_in, mate_slow)
        load_dy.wait()
        load_gate.wait()
        load_up.wait()

        def body(c, carry):
            going(c).wait_recv()
            hid, back = section_one_rows(
                x[span(c), :].astype(f32), dy[span(c, rows), :].astype(f32),
                dh[span(c), :],
                gate[...], up[...],
            )
            hidden[span(c, rows), :] = hid
            back_rows[span(c), :] = back
            coming(c).start()
            return carry

        lax.fori_loop(0, count, body, 0)

    @pl.when(section == 0)
    def _():
        keep(dy_in, dy)
        for piece in range(SLOW_PIECES):
            slow_pass(piece)
        for c in range(count):
            coming(c).wait_recv()

    for load in load_states:
        load.wait()
    wide = grad.shape[1]

    def begin(part, pair, order):
        c = part * (wide // width) + 2 * pair + order
        p = pl.ds(pl.multiple_of(c * width, width), width)
        local = pl.ds(pl.multiple_of((2 * pair + order) * width, width), width)

        def stage(q):
            g = grad[q, local]
            first = 0.9 * first_in[q, p].astype(f32) + 0.1 * g
            second = 0.999 * second_in[q, p].astype(f32) + 0.001 * g * g
            step = first / (jnp.sqrt(second) + 1e-08)
            own[c, q, :] = (step + 0.1 * slow[q, p].astype(f32)).astype(bf16)

        by_blocks(units, 128, stage)
        near_copy(c, order).start()

    def finish(c, order):
        p = pl.ds(pl.multiple_of(c * width, width), width)
        far_copy(c, order).wait_recv()

        def stage(q):
            mean = mean_of(c, order, q)
            moment = 0.9 * momentum[q, p].astype(f32) + mean
            averaged = 0.5 * (slow[q, p].astype(f32) + mate_slow[q, p].astype(f32))
            new_slow[q, p] = (averaged - 0.014 * (0.9 * moment + mean)).astype(bf16)
            new_momentum[q, p] = moment.astype(bf16)

        by_blocks(units, 128, stage)
        near_copy(c, order).wait_send()
        far_copy(c, order).wait_send()

    def run_part(part, carry):
        columns = pl.ds(pl.multiple_of(part * wide, wide), wide)
        grad[...] = grad_rows(dy[:, columns], hidden[...], units)

        def run_pair(pair, carry):
            for order in range(2):
                begin(part, pair, order)
            return carry

        return lax.fori_loop(0, wide // (2 * width), run_pair, carry)

    lax.fori_loop(0, model_width // wide, run_part, 0)
    every(pass_on)

    @pl.when(section == 0)
    def _():
        slow_finish()
        for c in range(count):
            going(c).wait_send()

    @pl.when(section == 1)
    def _():
        for c in range(count):
            coming(c).wait_send()

    every(finish)


def second_trip(
    flip, chunk, bits, ends, gate_w, up_w, first_in, second_in, momentum,
    slow, mate, hidden, dy, sent, dh,
):
    model_width, units = gate_w.shape
    rows = ends.shape[0] // 2
    count = rows // chunk
    width = 128
    chunks = model_width // width
    bf16, f32 = jnp.bfloat16, jnp.float32
    block = (chunks, units, width)
    outs = [jax.ShapeDtypeStruct(slow.shape, bf16)] * 2
    in_vmem = pl.BlockSpec(memory_space=pltpu.VMEM)
    dma = pltpu.SemaphoreType.DMA
    return pl.pallas_call(
        functools.partial(second_kernel, flip, chunk),
        out_shape=outs,
        in_specs=[pl.BlockSpec(memory_space=pltpu.SMEM)]
        + [pl.BlockSpec(memory_space=pltpu.HBM)] * 6
        + [in_vmem] * 6,
        out_specs=[in_vmem] * len(outs),
        scratch_shapes=[
            pltpu.VMEM(block, bf16), pltpu.VMEM(slow.shape, bf16),
            pltpu.VMEM(gate_w.shape, bf16), pltpu.VMEM(up_w.shape, bf16),
            *[pltpu.VMEM(slow.shape, bf16)] * 3,
            pltpu.VMEM((rows, model_width), bf16), pltpu.VMEM((rows, model_width), bf16),
            pltpu.VMEM((2 * rows, units), bf16), pltpu.VMEM((2 * rows, model_width), bf16),
            pltpu.VMEM((units, model_width // 2), f32),
            *slow_scratch(slow), *[pltpu.VMEM(block, bf16)] * 3,
            dma((5,)), dma, *[dma((count,))] * 4, *slow_semaphores(), *[dma((chunks,))] * 4,
        ],
        compiler_params=pltpu.CompilerParams(
            collective_id=16 + flip, has_side_effects=True, vmem_limit_bytes=14 * 1024 * 1024
        ),
        name="second",
    )(
        bits, ends, gate_w, up_w, first_in, second_in, momentum,
        slow, mate, hidden, dy, sent, dh,
    )


def last_kernel(new_slow, new_momentum, new_slow_h, new_momentum_h, sems):
    puts = (
        pltpu.make_async_copy(new_slow, new_slow_h, sems.at[0]),
        pltpu.make_async_copy(new_momentum, new_momentum_h, sems.at[1]),
    )
    for put in puts:
        put.start()
    for put in puts:
        put.wait()


def last_step(new_slow, new_momentum):
    out = jax.ShapeDtypeStruct(new_slow.shape, jnp.bfloat16)
    in_vmem = pl.BlockSpec(memory_space=pltpu.VMEM)
    in_hbm = pl.BlockSpec(memory_space=pltpu.HBM)
    return pl.pallas_call(
        last_kernel,
        out_shape=(out, out),
        in_specs=[in_vmem] * 2,
        out_specs=(in_hbm, in_hbm),
        scratch_shapes=[pltpu.SemaphoreType.DMA((2,))],
        compiler_params=pltpu.CompilerParams(vmem_limit_bytes=8 * 1024 * 1024),
        name="last",
    )(new_slow, new_momentum)


def trip_on_device(ends, w_gate, w_up, slow_down, adam_m, adam_v, momentum, routes, partner):
    micro_count, row_count, model_width = ends.shape[2:]
    flat_ends = ends.reshape(micro_count * row_count, model_width)
    gate_w, up_w, down_w = w_gate[0, 0], w_up[0, 0], slow_down[0, 0]
    chunk = row_count // 2
    flips = range(1, lax.axis_size("rep"))
    states = (adam_m[0, 0], adam_v[0, 0], momentum[0, 0])
    *keys, bits = read_keys(routes, partner)
    slow_v, mate_slow, hidden, dy, sent, dh = lax.switch(
        keys[0][0],
        [functools.partial(first_trip, flip, chunk) for flip in flips],
        bits, flat_ends, gate_w, up_w, down_w, *states,
    )
    new_slow, new_momentum = lax.switch(
        keys[1][0],
        [functools.partial(second_trip, flip, chunk) for flip in flips],
        bits, flat_ends, gate_w, up_w, *states,
        slow_v, mate_slow, hidden, dy, sent, dh,
    )
    new_slow, new_momentum = last_step(new_slow, new_momentum)
    return new_slow[None, None], new_momentum[None, None]


def wide_on_device(ends, w_gate, w_up, slow_down, adam_m, adam_v, momentum, routes, partner):
    micro_count, row_count, model_width = ends.shape[2:]
    own_data = ends.reshape(micro_count * row_count, model_width)
    gate_w = w_gate[0, 0]
    up_w = w_up[0, 0]
    down_w = slow_down[0, 0]
    hidden_units = gate_w.shape[1]
    replica = lax.axis_index("rep")
    on_first = lax.axis_index("section") == 0
    flip_keys = routes[:, 0]
    flip_bits = jnp.bitwise_xor(partner[replica], replica)
    near_slow = partner_2(down_w, "rep", 0)

    def cut(rows):
        return rows.reshape(micro_count, row_count, model_width)

    def first_forward():
        result, saved = forward_rows(own_data, gate_w, up_w, down_w)
        return result, saved[3]

    def first_idle():
        return own_data, jnp.zeros((own_data.shape[0], hidden_units), jnp.bfloat16)

    sent, hidden = lax.cond(on_first, first_forward, first_idle)
    sent = cut(sent)
    arrived = [send_rows(sent[b], flip_keys[b], 0) for b in range(micro_count)]
    near_slow, *arrived = lax.optimization_barrier((near_slow, *arrived))
    arrived = jnp.concatenate(arrived)
    chosen_slow = jnp.where(flip_bits & 1 == 1, near_slow, down_w)
    far_slow = partner_2(chosen_slow, "rep", 1)

    def last_work():
        _, saved = forward_rows(arrived, gate_w, up_w, down_w)
        term, back = backward_rows(own_data, arrived, saved, gate_w, up_w, down_w)
        return term, back

    def last_idle():
        return jnp.zeros((hidden_units, model_width), jnp.float32), own_data

    last_term, back = lax.cond(on_first, last_idle, last_work)
    back = cut(back)
    returned = [send_rows(back[b], flip_keys[b], 1) for b in range(micro_count)]
    far_slow, *returned = lax.optimization_barrier((far_slow, *returned))
    returned = jnp.concatenate(returned)
    partner_slow = jnp.where(flip_bits >> 1 & 1 == 1, far_slow, chosen_slow)
    grad_sum = lax.cond(
        on_first, lambda: grad_rows(returned, hidden, hidden_units), lambda: last_term
    )
    masks = jnp.zeros((8, model_width), jnp.int32)
    masks = masks.at[0].set(flip_bits & 1).at[1].set(flip_bits >> 1 & 1)
    new_slow, new_momentum = outer_update(
        masks, grad_sum, adam_m[0, 0], adam_v[0, 0], down_w, partner_slow, momentum[0, 0]
    )
    return new_slow[None, None], new_momentum[None, None]


def solution(mesh):
    weights = P("section", "rep", None, None)
    placed = (P("section", "rep", None, None, None),) + (weights,) * 6 + (P(), P())
    narrow = mesh.shape["rep"] <= 16
    on_device = trip_on_device if narrow else wide_on_device

    return jax.shard_map(
        on_device, mesh=mesh, in_specs=placed, out_specs=(weights, weights), check_vma=False
    )
```
